256 devices in a mesh: bulk: 8 (over x, core), own: 32 (over y, z).
Axes of the slice: x: 4, y: 4, z: 8, core: 2. Of those that a mesh axis runs over, the one named last changes fastest.
Arguments:
- velocity: float32 [3, 8, 32, 96, 5832], P(None, 'bulk', 'own'), may hold values from -6 to 6
- new_owner: int32 [8, 32, 96], P('bulk', 'own'), may hold values from 0 to 31, as said below
- box_block: int32 [8, 32, 96], P('bulk', 'own'), may hold values from 0 to 383, as said below
- box_count: int32 [8, 32], P('bulk', 'own'), may hold values from 0 to 96, as said below
- box_level: int32 [8, 32, 96], P('bulk', 'own'), may hold values from 1 to 3
Outputs:
- cosine_part: float32 [32, 256, 3072], P('own', 'bulk')
- sine_part: float32 [32, 256, 3072], P('own', 'bulk')
The draws below stay inside these ranges and needn't reach their ends.
Inputs may be any that keep to these rules, and one draw needn't show every extreme that they name: `new_owner`: at each bulk index b, the live slots that name new owner r number exactly 48 in all, and one old device gives either none or exactly 3 of them to one new owner. `box_block`: A live slot at bulk index b names a block from b * 48 to (b + 1) * 48 - 1, and the live slots at b that name one new owner name each of these blocks once. The live slots of an old device are its slots 0 to box_count - 1. At every bulk index some old device has all 96 slots live and some has none.
All inputs are finite; a program needn't handle non-finite values.
Results may differ from the reference program's by a relative error of at most 0.0003.
Values sent between devices are 32-bit elements; how exact they have to be, the bound alone decides.
A program may use at most 128 MiB of HBM per device.

```python
import math
import jax
import jax.numpy as jnp
from jax import lax

BOX = 16
CELLS = 5832
NX = 6144
HALF = 3072
BLOCKS = 384
SLOTS = 96
N_BULK = 8
N_OWN = 32


def layout_group(group_key, group_index):
    window = N_OWN // 2
    held_blocks = BLOCKS // N_BULK
    per_pair = 2 * held_blocks // N_OWN
    slot_total = 2 * held_blocks
    hot_key = jax.random.fold_in(group_key, 1)
    start_key = jax.random.fold_in(group_key, 2)
    block_key = jax.random.fold_in(group_key, 3)
    order_key = jax.random.fold_in(group_key, 4)
    hot_owner = jax.random.randint(hot_key, (), 0, N_OWN)
    starts = hot_owner - jax.random.randint(start_key, (N_OWN,), 0, window)
    block_orders = jax.vmap(lambda row_key: jax.random.permutation(row_key, held_blocks))(jax.random.split(block_key, N_OWN))
    old_ids = jnp.arange(N_OWN)[:, None, None]
    target_ids = jnp.broadcast_to(jnp.arange(N_OWN)[None, :, None], (N_OWN, N_OWN, per_pair))
    within = jnp.arange(per_pair)[None, None, :]
    offset = (old_ids - starts[None, :, None]) % N_OWN
    covered = jnp.broadcast_to(offset < window, (N_OWN, N_OWN, per_pair))
    pick_index = jnp.minimum(offset, window - 1) * per_pair + within
    blocks = block_orders[target_ids, pick_index] + group_index * held_blocks
    flat_live = covered.reshape(N_OWN, slot_total).astype(jnp.int32)
    flat_owner = target_ids.reshape(N_OWN, slot_total)
    flat_block = blocks.reshape(N_OWN, slot_total)
    shuffles = jax.vmap(lambda row_key: jax.random.permutation(row_key, slot_total))(jax.random.split(order_key, N_OWN))
    sort_score = (1 - flat_live) * slot_total + shuffles
    slot_order = jnp.argsort(sort_score, axis=1)
    owner_rows = jnp.take_along_axis(flat_owner, slot_order, axis=1)
    block_rows = jnp.take_along_axis(flat_block, slot_order, axis=1)
    count_rows = jnp.sum(flat_live, axis=1)
    return (owner_rows.astype(jnp.int32), block_rows.astype(jnp.int32), count_rows.astype(jnp.int32))


def draw_layout(key):
    base_key = jax.random.fold_in(key, 7)
    group_ids = jnp.arange(N_BULK)
    return jax.vmap(lambda group_index: layout_group(jax.random.fold_in(base_key, group_index), group_index))(group_ids)


def draw_new_owner(key, part):
    return draw_layout(key)[0]


def draw_box_block(key, part):
    return draw_layout(key)[1]


def draw_box_count(key, part):
    return draw_layout(key)[2]


def touch_ends(entries, rng, low, top_value):
    index_at = [jax.random.randint(jax.random.fold_in(rng, axis), (), 0, length) for axis, length in enumerate(entries.shape)]
    widest = entries.shape.index(max(entries.shape))
    beside = index_at[:widest] + [(index_at[widest] + 1) % entries.shape[widest]] + index_at[widest + 1:]
    return entries.at[tuple(index_at)].set(low).at[tuple(beside)].set(top_value)


def block_scale(rng, extent, shards, least, top_value):
    def one(axis_at, blocks):
        steps = jax.random.uniform(jax.random.fold_in(jax.random.fold_in(rng, 6), axis_at), (blocks,), jnp.float32, least / len(shards), top_value / len(shards))
        return jnp.repeat(jnp.exp(steps), extent[axis_at] // blocks).reshape((-1,) + (1,) * (len(extent) - axis_at - 1))

    factor_of = one(*shards[0])
    for cut in shards[1:]:
        factor_of = factor_of * one(*cut)
    return factor_of


def gaussian(key, shape, spread, most, cuts=(), held_as=jnp.bfloat16):
    factor_of = block_scale(key, shape, cuts, -0.22, 0.18) if cuts else 1.0
    drawn = jax.random.normal(key, shape, jnp.float32) * spread * factor_of
    return jnp.minimum(jnp.maximum(drawn, -most), most).astype(held_as)


def setup_inputs(seed: int = 0) -> dict:
    arg_keys = jax.random.split(jax.random.key(seed), 6)
    return {
        "velocity": gaussian(arg_keys[0], (3, N_BULK, N_OWN, SLOTS, CELLS), 1.0, 6.0, ((1, 8), (2, 32)), jnp.float32),
        "new_owner": draw_new_owner(jax.random.fold_in(arg_keys[5], 71), 0),
        "box_block": draw_box_block(jax.random.fold_in(arg_keys[5], 71), 0),
        "box_count": draw_box_count(jax.random.fold_in(arg_keys[5], 71), 0),
        "box_level": touch_ends(jax.random.randint(arg_keys[4], (N_BULK, N_OWN, SLOTS), 1, 4), jax.random.fold_in(arg_keys[4], 1), 1, 3).astype(jnp.int32),
    }


def level_factor(level):
    return jnp.where(level == 1, 0.5, jnp.where(level == 2, 1.0, 2.0)).astype(jnp.float32)

def cube_divergence(fields, factor):
    box_total = fields.shape[1]
    ghosted = BOX + 2
    cubes = fields.reshape(3, box_total, ghosted, ghosted, ghosted)
    streamwise = cubes[0]
    spanwise = cubes[1]
    vertical = cubes[2]
    along_x = streamwise[:, 1:-1, 1:-1, 2:] - streamwise[:, 1:-1, 1:-1, :-2]
    along_y = spanwise[:, 2:, 1:-1, 1:-1] - spanwise[:, :-2, 1:-1, 1:-1]
    along_z = vertical[:, 1:-1, 2:, 1:-1] - vertical[:, 1:-1, :-2, 1:-1]
    return factor[:, None, None, None] * (along_x + (along_y + along_z))

def reference(velocity, new_owner, box_block, box_count, box_level):

    def group_divergence(group_index):
        fields = lax.dynamic_index_in_dim(velocity, group_index, 1, keepdims=False)
        levels_here = lax.dynamic_index_in_dim(box_level, group_index, 0, keepdims=False)
        return cube_divergence(fields.reshape(3, N_OWN * SLOTS, CELLS), level_factor(levels_here.reshape(-1)))
    divergence = lax.map(group_divergence, jnp.arange(N_BULK, dtype=jnp.int32))
    slot_ids = jnp.arange(SLOTS, dtype=jnp.int32)
    filled = slot_ids[None, None, :] < box_count[:, :, None]
    target = jnp.where(filled, new_owner * BLOCKS + box_block, N_OWN * BLOCKS).reshape(-1).astype(jnp.int32)
    placed = jnp.zeros((N_OWN * BLOCKS, BOX, BOX, BOX), divergence.dtype)
    placed = placed.at[target].set(divergence.reshape(-1, BOX, BOX, BOX), mode='drop')
    pencil = placed.reshape(N_OWN, BLOCKS, BOX, BOX, BOX).transpose(0, 2, 3, 1, 4).reshape(N_OWN, BOX * BOX, NX)
    norm_scale = 1.0 / math.sqrt(NX)

    def owner_spectra(rows_here):
        spectrum = jnp.fft.rfft(rows_here, axis=-1)[..., :HALF]
        return (jnp.real(spectrum) * norm_scale, -jnp.imag(spectrum) * norm_scale)
    cosine_part, sine_part = lax.map(owner_spectra, pencil)
    return (cosine_part, sine_part)
```

```python
import math

import numpy as np

import jax
import jax.numpy as jnp
from jax import lax
from jax.experimental import pallas as pl
from jax.experimental.pallas import tpu as pltpu
from jax.sharding import PartitionSpec as P

BOX = 16
GHOST = BOX + 2
PLANE = GHOST * GHOST
PLANE_PAD = 384
FACE = BOX * BOX
HALF = 3072
NX = 6144
SUB = 16
CODE_W = 256

HIGHEST = lax.Precision.HIGHEST
F32 = jnp.float32
BF16 = jnp.bfloat16


def level_factor(level):
    return jnp.where(level == 1, 0.5, jnp.where(level == 2, 1.0, 2.0)).astype(jnp.float32)


def stencil_tables():
    dx = np.zeros((PLANE_PAD, FACE), np.float32)
    dz = np.zeros((PLANE_PAD, FACE), np.float32)
    sel = np.zeros((PLANE_PAD, FACE), np.float32)
    for j in range(BOX):
        for k in range(BOX):
            q = j * BOX + k
            dx[GHOST * (j + 1) + k + 2, q] += 1.0
            dx[GHOST * (j + 1) + k, q] -= 1.0
            dz[GHOST * (j + 2) + k + 1, q] += 1.0
            dz[GHOST * j + k + 1, q] -= 1.0
            sel[GHOST * (j + 1) + k + 1, q] = 1.0
    return (jnp.asarray(dx, BF16), jnp.asarray(dz, BF16), jnp.asarray(sel, BF16))


def _split2(x):
    hi = x.astype(BF16)
    lo = (x - hi.astype(F32)).astype(BF16)
    return hi, lo


def _mm2(x, m):
    hi, lo = _split2(x)
    return jnp.dot(hi, m, preferred_element_type=F32) + jnp.dot(lo, m, preferred_element_type=F32)


def _mm3_left(p, x):
    hi = x.astype(BF16)
    rest = x - hi.astype(F32)
    mid = rest.astype(BF16)
    lo = (rest - mid.astype(F32)).astype(BF16)
    return (
        jnp.dot(p, hi, preferred_element_type=F32)
        + jnp.dot(p, mid, preferred_element_type=F32)
        + jnp.dot(p, lo, preferred_element_type=F32)
    )


def divergence_kernel(u_ref, w_ref, v0_ref, v2_ref, dx_ref, dz_ref, sel_ref, p_ref, code_ref, o_ref):
    i = pl.program_id(0)

    @pl.when(i < BOX)
    def _():
        along_x = _mm2(u_ref[0], dx_ref[...])
        along_y = _mm2(v2_ref[0] - v0_ref[0], sel_ref[...])
        along_z = _mm2(w_ref[0], dz_ref[...])
        o_ref[...] = _mm3_left(p_ref[...], along_x + (along_y + along_z))

    @pl.when(i == BOX)
    def _():
        o_ref[...] = code_ref[...]


def source_divergence(planes, permute, codes):
    slots = planes.shape[2]
    dx, dz, sel = stencil_tables()
    last = GHOST - 1
    plane_spec = lambda shift: pl.BlockSpec(
        (1, slots, PLANE_PAD), lambda i: (jnp.minimum(i + shift, last), 0, 0)
    )
    table_spec = pl.BlockSpec((PLANE_PAD, FACE), lambda i: (0, 0))
    return pl.pallas_call(
        divergence_kernel,
        grid=(BOX + 1,),
        in_specs=[
            plane_spec(1),
            plane_spec(1),
            plane_spec(0),
            plane_spec(2),
            table_spec,
            table_spec,
            table_spec,
            pl.BlockSpec((slots, slots), lambda i: (0, 0)),
            pl.BlockSpec((slots, CODE_W), lambda i: (0, 0)),
        ],
        out_specs=pl.BlockSpec((slots, FACE), lambda i: (0, i)),
        out_shape=jax.ShapeDtypeStruct((slots, (BOX + 1) * FACE), F32),
        cost_estimate=pl.CostEstimate(
            flops=2 * slots * PLANE_PAD * FACE * 6 * BOX + 2 * slots * slots * FACE * 3 * BOX,
            bytes_accessed=4 * (4 * BOX * slots * PLANE_PAD + slots * (BOX + 1) * FACE),
            transcendentals=0,
        ),
    )(planes[0], planes[2], planes[1], planes[1], dx, dz, sel, permute, codes)


def angle_cos_sin(product, period):
    angles = (2.0 * math.pi / period) * (product % period).astype(F32)
    return jnp.cos(angles), jnp.sin(angles)


def line_spectra(x):
    blocks, width = x.shape
    lines = width // SUB
    f2_total = HALF // blocks
    g_ids = jnp.arange(blocks, dtype=jnp.int32)
    c1, s1 = angle_cos_sin(g_ids[:, None] * g_ids[None, :], blocks)
    dims = (((0,), (0,)), ((), ()))
    y_re = lax.dot_general(x, c1, dims, precision=HIGHEST)
    y_im = -lax.dot_general(x, s1, dims, precision=HIGHEST)
    k_of = jnp.arange(width, dtype=jnp.int32) % SUB
    tw_c, tw_s = angle_cos_sin(k_of[:, None] * g_ids[None, :], NX)
    z_re = y_re * tw_c + y_im * tw_s
    z_im = y_im * tw_c - y_re * tw_s
    row = jnp.arange(lines * f2_total, dtype=jnp.int32)
    col = jnp.arange(width, dtype=jnp.int32)
    same_line = (row[:, None] // f2_total) == (col[None, :] // SUB)
    bd_c, bd_s = angle_cos_sin((row[:, None] % f2_total) * (col[None, :] % SUB), SUB)
    bd_c = jnp.where(same_line, bd_c, 0.0)
    bd_s = jnp.where(same_line, bd_s, 0.0)
    x_re = jnp.dot(bd_c, z_re, precision=HIGHEST) + jnp.dot(bd_s, z_im, precision=HIGHEST)
    x_im = jnp.dot(bd_c, z_im, precision=HIGHEST) - jnp.dot(bd_s, z_re, precision=HIGHEST)
    norm_scale = 1.0 / math.sqrt(NX)
    cosine = x_re.reshape(lines, HALF) * norm_scale
    sine_vals = -x_im.reshape(lines, HALF) * norm_scale
    return cosine, sine_vals


def body(velocity, new_owner, box_block, box_count, box_level):
    owners = lax.axis_size("own")
    groups = lax.axis_size("bulk")
    slot_total = velocity.shape[3]
    per_pair = slot_total // owners
    parcel_rows = owners * per_pair
    held_blocks = slot_total // 2
    first_block = lax.axis_index("bulk") * held_blocks
    slot_ids = jnp.arange(slot_total, dtype=jnp.int32)
    destination = new_owner[0, 0]
    filled = slot_ids < box_count[0, 0]
    owner_hits = (
        filled[:, None] & (destination[:, None] == jnp.arange(owners, dtype=jnp.int32)[None, :])
    ).astype(jnp.int32)
    earlier = jnp.cumsum(owner_hits, axis=0) - owner_hits
    order_rank = jnp.sum(earlier * owner_hits, axis=1)
    position = jnp.where(filled, destination * per_pair + order_rank, parcel_rows)
    parcel_ids = jnp.arange(parcel_rows, dtype=jnp.int32)
    factor = level_factor(box_level[0, 0])
    permute = jnp.where(position[None, :] == parcel_ids[:, None], factor[None, :], 0.0).astype(BF16)
    source = jnp.full((parcel_rows,), slot_total, jnp.int32).at[position].set(slot_ids, mode="drop")
    occupied = source < slot_total
    source_safe = jnp.minimum(source, slot_total - 1)
    blocks_out = jnp.where(occupied, jnp.take(box_block[0, 0], source_safe), -1).astype(F32)
    codes = jnp.broadcast_to(blocks_out[:, None], (parcel_rows, CODE_W))

    cells = velocity[:, 0, 0].reshape(3, slot_total, GHOST, PLANE)
    cells = jnp.pad(cells, ((0, 0), (0, 0), (0, 0), (0, PLANE_PAD - PLANE)))
    planes = jnp.transpose(cells, (0, 2, 1, 3))
    parcel = source_divergence(planes, permute, codes)

    arrived = lax.all_to_all(parcel, "own", split_axis=0, concat_axis=0, tiled=True)
    code_in = arrived[:, BOX * FACE]
    place_at = jnp.where(code_in >= 0, code_in.astype(jnp.int32) - first_block, held_blocks)
    chosen = jnp.zeros((held_blocks,), jnp.int32).at[place_at].set(parcel_ids, mode="drop")
    rows_per_group = BOX * FACE // groups
    column = arrived[:, : BOX * FACE].reshape(parcel_rows, groups, rows_per_group)
    outgoing = jnp.transpose(jnp.take(column, chosen, axis=0), (1, 0, 2))
    gathered = lax.all_to_all(outgoing, "bulk", split_axis=0, concat_axis=0, tiled=True)
    cosine, sine_vals = line_spectra(gathered.reshape(groups * held_blocks, rows_per_group))
    return (cosine[None], sine_vals[None])


def solution(mesh):
    in_specs = (
        P(None, "bulk", "own", None, None),
        P("bulk", "own", None),
        P("bulk", "own", None),
        P("bulk", "own"),
        P("bulk", "own", None),
    )
    out_specs = (P("own", "bulk", None), P("own", "bulk", None))
    return jax.shard_map(body, mesh=mesh, in_specs=in_specs, out_specs=out_specs, check_vma=False)
```

```python
import math

import numpy as np

import jax
import jax.numpy as jnp
from jax import lax
from jax.experimental import pallas as pl
from jax.experimental.pallas import tpu as pltpu
from jax.sharding import PartitionSpec as P

BOX = 16
GHOST = BOX + 2
PLANE = GHOST * GHOST
PLANE_PAD = 384
FACE = BOX * BOX
HALF = 3072
NX = 6144
SUB = 16
CODE_W = 256

HIGHEST = lax.Precision.HIGHEST
F32 = jnp.float32
BF16 = jnp.bfloat16


def level_factor(level):
    return jnp.where(level == 1, 0.5, jnp.where(level == 2, 1.0, 2.0)).astype(jnp.float32)


def selection_table():
    sel = np.zeros((PLANE_PAD, FACE), np.float32)
    for j in range(BOX):
        for k in range(BOX):
            sel[GHOST * (j + 1) + k + 1, j * BOX + k] = 1.0
    return jnp.asarray(sel, BF16)


def _split2(x):
    hi = x.astype(BF16)
    lo = (x - hi.astype(F32)).astype(BF16)
    return hi, lo


def _split3(x):
    hi = x.astype(BF16)
    rest = x - hi.astype(F32)
    mid = rest.astype(BF16)
    lo = (rest - mid.astype(F32)).astype(BF16)
    return hi, mid, lo


def _dot(a, b):
    return jnp.dot(a, b, preferred_element_type=F32)


def _exact_right(x, m):
    hi, mid, lo = _split3(x)
    return _dot(hi, m) + _dot(mid, m) + _dot(lo, m)


def _exact_left(m, x):
    hi, mid, lo = _split3(x)
    return _dot(m, hi) + _dot(m, mid) + _dot(m, lo)


WINDOW = 512
ROW_PAD = 6016


def _plane(x_ref, field, p):
    start = PLANE * p
    base = (start // 128) * 128
    off = start - base
    w = x_ref[field, :, base:base + WINDOW]
    if off:
        w = pltpu.roll(w, WINDOW - off, 1)
    return w[:, :PLANE_PAD]


def divergence_kernel(x_ref, sel_ref, p_ref, code_ref, o_ref):
    h = pl.program_id(0)
    pieces = []
    for i in range(BOX):
        u = _plane(x_ref, 0, i + 1)
        w = _plane(x_ref, 2, i + 1)
        along_x = pltpu.roll(u, PLANE_PAD - 1, 1) - pltpu.roll(u, 1, 1)
        along_y = _plane(x_ref, 1, i + 2) - _plane(x_ref, 1, i)
        along_z = pltpu.roll(w, PLANE_PAD - GHOST, 1) - pltpu.roll(w, GHOST, 1)
        pieces.append(along_x + (along_y + along_z))
    interior = _exact_right(jnp.concatenate(pieces, axis=0), sel_ref[...])
    rows = p_ref.shape[2]
    permute = p_ref[0]

    @pl.when(h == 0)
    def _():
        o_ref[...] = jnp.zeros_like(o_ref)
        o_ref[:, BOX * FACE:] = code_ref[...]

    for i in range(BOX):
        o_ref[:, i * FACE:(i + 1) * FACE] += _exact_left(permute, interior[i * rows:(i + 1) * rows])


def source_divergence(flat, permute, codes, halves=2):
    slots = flat.shape[1]
    part = slots // halves
    sel = selection_table()
    return pl.pallas_call(
        divergence_kernel,
        grid=(halves,),
        in_specs=[
            pl.BlockSpec((3, part, ROW_PAD), lambda h: (0, h, 0)),
            pl.BlockSpec((PLANE_PAD, FACE), lambda h: (0, 0)),
            pl.BlockSpec((1, slots, part), lambda h: (h, 0, 0)),
            pl.BlockSpec((slots, CODE_W), lambda h: (0, 0)),
        ],
        out_specs=pl.BlockSpec((slots, BOX * FACE + CODE_W), lambda h: (0, 0)),
        out_shape=jax.ShapeDtypeStruct((slots, BOX * FACE + CODE_W), F32),
        cost_estimate=pl.CostEstimate(
            flops=2 * slots * BOX * PLANE_PAD * FACE * 3 + 2 * slots * slots * BOX * FACE * 3,
            bytes_accessed=4 * (3 * slots * ROW_PAD + slots * (BOX * FACE + CODE_W)),
            transcendentals=0,
        ),
    )(flat, sel, jnp.transpose(permute.reshape(slots, halves, part), (1, 0, 2)), codes)


def angle_cos_sin(product, period):
    angles = (2.0 * math.pi / period) * (product % period).astype(F32)
    return jnp.cos(angles), jnp.sin(angles)


def _split_table(t):
    hi = lax.reduce_precision(t, exponent_bits=8, mantissa_bits=7)
    return hi.astype(BF16), (t - hi).astype(BF16)


def _mm3(a_hi, a_lo, b_hi, b_lo, dims=None):
    if dims is None:
        f = _dot
    else:
        f = lambda a, b: lax.dot_general(a, b, dims, preferred_element_type=F32)
    return f(a_hi, b_hi) + (f(a_hi, b_lo) + f(a_lo, b_hi))


NT = (((1,), (1,)), ((), ()))


def dft_kernel(x_ref, c1h, c1l, s1h, s1l, twc_ref, tws_ref, bch, bcl, bsh, bsl, cos_ref, sin_ref):
    xh, xl = _split2(x_ref[...])
    y_re = _mm3(c1h[...], c1l[...], xh, xl)
    y_im = -_mm3(s1h[...], s1l[...], xh, xl)
    twc = twc_ref[...]
    tws = tws_ref[...]
    z_re = y_re * twc + y_im * tws
    z_im = y_im * twc - y_re * tws
    zrh, zrl = _split2(z_re)
    zih, zil = _split2(z_im)
    bc_h, bc_l, bs_h, bs_l = bch[...], bcl[...], bsh[...], bsl[...]
    x_re = _mm3(bc_h, bc_l, zrh, zrl, NT) + _mm3(bs_h, bs_l, zih, zil, NT)
    x_neg_im = _mm3(bs_h, bs_l, zrh, zrl, NT) - _mm3(bc_h, bc_l, zih, zil, NT)
    norm_scale = 1.0 / math.sqrt(NX)
    lines = cos_ref.shape[0]
    blocks = x_ref.shape[0]
    for f2 in range(cos_ref.shape[1] // blocks):
        cos_ref[:, f2 * blocks:(f2 + 1) * blocks] = x_re[f2 * lines:(f2 + 1) * lines] * norm_scale
        sin_ref[:, f2 * blocks:(f2 + 1) * blocks] = x_neg_im[f2 * lines:(f2 + 1) * lines] * norm_scale


def line_spectra(x):
    blocks, width = x.shape
    lines = width // SUB
    f2_total = HALF // blocks
    g_ids = jnp.arange(blocks, dtype=jnp.int32)
    c1, s1 = angle_cos_sin(g_ids[:, None] * g_ids[None, :], blocks)
    k_of = jnp.arange(width, dtype=jnp.int32) % SUB
    tw_c, tw_s = angle_cos_sin(g_ids[:, None] * k_of[None, :], NX)
    row = jnp.arange(lines * f2_total, dtype=jnp.int32)
    col = jnp.arange(width, dtype=jnp.int32)
    same_line = (row[:, None] % lines) == (col[None, :] // SUB)
    bd_c, bd_s = angle_cos_sin((row[:, None] // lines) * (col[None, :] % SUB), SUB)
    bd_c = jnp.where(same_line, bd_c, 0.0)
    bd_s = jnp.where(same_line, bd_s, 0.0)
    tables = (*_split_table(c1), *_split_table(s1), tw_c, tw_s, *_split_table(bd_c), *_split_table(bd_s))
    out = jax.ShapeDtypeStruct((lines, HALF), F32)
    return pl.pallas_call(
        dft_kernel,
        out_shape=(out, out),
        cost_estimate=pl.CostEstimate(
            flops=2 * 3 * (2 * blocks * blocks * width + 4 * lines * f2_total * width * blocks),
            bytes_accessed=4 * (blocks * width * 3 + 2 * lines * HALF) + 2 * (4 * blocks * blocks + 4 * lines * f2_total * width),
            transcendentals=0,
        ),
    )(x, *tables)


def body(velocity, new_owner, box_block, box_count, box_level):
    owners = lax.axis_size("own")
    groups = lax.axis_size("bulk")
    slot_total = velocity.shape[3]
    per_pair = slot_total // owners
    parcel_rows = owners * per_pair
    held_blocks = slot_total // 2
    first_block = lax.axis_index("bulk") * held_blocks
    slot_ids = jnp.arange(slot_total, dtype=jnp.int32)
    destination = new_owner[0, 0]
    filled = slot_ids < box_count[0, 0]
    owner_hits = (
        filled[:, None] & (destination[:, None] == jnp.arange(owners, dtype=jnp.int32)[None, :])
    ).astype(jnp.int32)
    earlier = jnp.cumsum(owner_hits, axis=0) - owner_hits
    order_rank = jnp.sum(earlier * owner_hits, axis=1)
    position = jnp.where(filled, destination * per_pair + order_rank, parcel_rows)
    parcel_ids = jnp.arange(parcel_rows, dtype=jnp.int32)
    factor = level_factor(box_level[0, 0])
    permute = jnp.where(position[None, :] == parcel_ids[:, None], factor[None, :], 0.0).astype(BF16)
    source = jnp.full((parcel_rows,), slot_total, jnp.int32).at[position].set(slot_ids, mode="drop")
    occupied = source < slot_total
    source_safe = jnp.minimum(source, slot_total - 1)
    blocks_out = jnp.where(occupied, jnp.take(box_block[0, 0], source_safe), -1).astype(F32)
    codes = jnp.broadcast_to(blocks_out[:, None], (parcel_rows, CODE_W))

    cells = velocity[:, 0, 0]
    flat = jnp.pad(cells, ((0, 0), (0, 0), (0, ROW_PAD - cells.shape[-1])))
    parcel = source_divergence(flat, permute, codes)

    arrived = lax.all_to_all(parcel, "own", split_axis=0, concat_axis=0, tiled=True)
    code_in = arrived[:, BOX * FACE]
    place_at = jnp.where(code_in >= 0, code_in.astype(jnp.int32) - first_block, held_blocks)
    chosen = jnp.zeros((held_blocks,), jnp.int32).at[place_at].set(parcel_ids, mode="drop")
    rows_per_group = BOX * FACE // groups
    column = arrived[:, : BOX * FACE].reshape(parcel_rows, groups, rows_per_group)
    outgoing = jnp.transpose(jnp.take(column, chosen, axis=0), (1, 0, 2))
    gathered = lax.all_to_all(outgoing, "bulk", split_axis=0, concat_axis=0, tiled=True)
    cosine, sine_vals = line_spectra(gathered.reshape(groups * held_blocks, rows_per_group))
    return (cosine[None], sine_vals[None])


def solution(mesh):
    in_specs = (
        P(None, "bulk", "own", None, None),
        P("bulk", "own", None),
        P("bulk", "own", None),
        P("bulk", "own"),
        P("bulk", "own", None),
    )
    out_specs = (P("own", "bulk", None), P("own", "bulk", None))
    return jax.shard_map(body, mesh=mesh, in_specs=in_specs, out_specs=out_specs, check_vma=False)
```

```python
import math

import ml_dtypes
import numpy as np

import jax
import jax.numpy as jnp
from jax import lax
from jax.experimental import pallas as pl
from jax.experimental.pallas import tpu as pltpu
from jax.sharding import PartitionSpec as P

BOX = 16
GHOST = BOX + 2
PLANE = GHOST * GHOST
PLANE_PAD = 384
FACE = BOX * BOX
HALF = 3072
NX = 6144
SUB = 16
CODE_W = 128

HIGHEST = lax.Precision.HIGHEST
F32 = jnp.float32
BF16 = jnp.bfloat16


def level_factor(level):
    return jnp.where(level == 1, 0.5, jnp.where(level == 2, 1.0, 2.0)).astype(jnp.float32)


def selection_table():
    sel = np.zeros((PLANE_PAD, FACE), np.float32)
    for j in range(BOX):
        for k in range(BOX):
            sel[GHOST * (j + 1) + k + 1, j * BOX + k] = 1.0
    return jnp.asarray(sel, BF16)


def _split2(x):
    hi = x.astype(BF16)
    lo = (x - hi.astype(F32)).astype(BF16)
    return hi, lo


def _split3(x):
    hi = x.astype(BF16)
    rest = x - hi.astype(F32)
    mid = rest.astype(BF16)
    lo = (rest - mid.astype(F32)).astype(BF16)
    return hi, mid, lo


def _dot(a, b):
    return jnp.dot(a, b, preferred_element_type=F32)


def _exact_right(x, m):
    hi, mid, lo = _split3(x)
    return _dot(hi, m) + _dot(mid, m) + _dot(lo, m)


def _exact_left(m, x):
    hi, mid, lo = _split3(x)
    return _dot(m, hi) + _dot(m, mid) + _dot(m, lo)


WINDOW = 512
ROW_PAD = 6016


def _plane(x_ref, field, p):
    start = PLANE * p
    base = (start // 128) * 128
    off = start - base
    w = x_ref[field, :, base:base + WINDOW]
    if off:
        w = pltpu.roll(w, WINDOW - off, 1)
    return w[:, :PLANE_PAD]


def divergence_kernel(x_ref, sel_ref, p_ref, code_ref, o_ref):
    h = pl.program_id(0)
    pieces = []
    for i in range(BOX):
        u = _plane(x_ref, 0, i + 1)
        w = _plane(x_ref, 2, i + 1)
        along_x = pltpu.roll(u, PLANE_PAD - 1, 1) - pltpu.roll(u, 1, 1)
        along_y = _plane(x_ref, 1, i + 2) - _plane(x_ref, 1, i)
        along_z = pltpu.roll(w, PLANE_PAD - GHOST, 1) - pltpu.roll(w, GHOST, 1)
        pieces.append(along_x + (along_y + along_z))
    interior = _exact_right(jnp.concatenate(pieces, axis=0), sel_ref[...])
    rows = p_ref.shape[2]
    permute = p_ref[0]

    @pl.when(h == 0)
    def _():
        o_ref[...] = jnp.zeros_like(o_ref)
        o_ref[:, BOX * FACE:] = code_ref[...]

    for i in range(BOX):
        o_ref[:, i * FACE:(i + 1) * FACE] += _exact_left(permute, interior[i * rows:(i + 1) * rows])


def source_divergence(flat, permute, codes, halves=2):
    slots = flat.shape[1]
    part = slots // halves
    sel = selection_table()
    return pl.pallas_call(
        divergence_kernel,
        grid=(halves,),
        in_specs=[
            pl.BlockSpec((3, part, ROW_PAD), lambda h: (0, h, 0)),
            pl.BlockSpec((PLANE_PAD, FACE), lambda h: (0, 0)),
            pl.BlockSpec((1, slots, part), lambda h: (h, 0, 0)),
            pl.BlockSpec((slots, CODE_W), lambda h: (0, 0)),
        ],
        out_specs=pl.BlockSpec((slots, BOX * FACE + CODE_W), lambda h: (0, 0)),
        out_shape=jax.ShapeDtypeStruct((slots, BOX * FACE + CODE_W), F32),
        cost_estimate=pl.CostEstimate(
            flops=2 * slots * BOX * PLANE_PAD * FACE * 3 + 2 * slots * slots * BOX * FACE * 3,
            bytes_accessed=4 * (3 * slots * ROW_PAD + slots * (BOX * FACE + CODE_W)),
            transcendentals=0,
        ),
    )(flat, sel, jnp.transpose(permute.reshape(slots, halves, part), (1, 0, 2)), codes)


def _split_np(t):
    hi = t.astype(ml_dtypes.bfloat16)
    lo = (t - hi.astype(np.float64)).astype(ml_dtypes.bfloat16)
    return jnp.asarray(hi), jnp.asarray(lo)


def _angles(product, period):
    return (2.0 * np.pi / period) * (product % period).astype(np.float64)


def dft_tables(blocks, lines_per_block, f2_total):
    g_ids = np.arange(blocks, dtype=np.int64)
    stage_one = _angles(g_ids[:, None] * g_ids[None, :], blocks)
    lanes = lines_per_block * SUB
    twist = _angles(g_ids[:, None] * (np.arange(lanes) % SUB)[None, :], NX)
    row = np.arange(f2_total * lines_per_block)
    col = np.arange(lanes)
    same_line = (row[:, None] % lines_per_block) == (col[None, :] // SUB)
    last = _angles((row[:, None] // lines_per_block) * (col[None, :] % SUB), SUB)
    return (
        *_split_np(np.cos(stage_one)),
        *_split_np(np.sin(stage_one)),
        jnp.asarray(np.cos(twist), F32),
        jnp.asarray(np.sin(twist), F32),
        *_split_np(np.where(same_line, np.cos(last), 0.0)),
        *_split_np(np.where(same_line, np.sin(last), 0.0)),
    )


def _mm3(a_hi, a_lo, b_hi, b_lo, dims=None):
    if dims is None:
        f = _dot
    else:
        f = lambda a, b: lax.dot_general(a, b, dims, preferred_element_type=F32)
    return f(a_hi, b_hi) + (f(a_hi, b_lo) + f(a_lo, b_hi))


NT = (((1,), (1,)), ((), ()))
LANE = 128


def dft_kernel(x_ref, c1h, c1l, s1h, s1l, twc_ref, tws_ref, bch, bcl, bsh, bsl, cos_ref, sin_ref):
    xh, xl = _split2(x_ref[...])
    y_re = _mm3(c1h[...], c1l[...], xh, xl)
    y_im = -_mm3(s1h[...], s1l[...], xh, xl)
    twc = twc_ref[...]
    tws = tws_ref[...]
    bc_h, bc_l, bs_h, bs_l = bch[...], bcl[...], bsh[...], bsl[...]
    norm_scale = 1.0 / math.sqrt(NX)
    blocks = x_ref.shape[0]
    lines_per_block = LANE // SUB
    for part in range(x_ref.shape[1] // LANE):
        cols = slice(part * LANE, (part + 1) * LANE)
        yr = y_re[:, cols]
        yi = y_im[:, cols]
        zrh, zrl = _split2(yr * twc + yi * tws)
        zih, zil = _split2(yi * twc - yr * tws)
        x_re = _mm3(bc_h, bc_l, zrh, zrl, NT) + _mm3(bs_h, bs_l, zih, zil, NT)
        x_neg_im = _mm3(bs_h, bs_l, zrh, zrl, NT) - _mm3(bc_h, bc_l, zih, zil, NT)
        rows = slice(part * lines_per_block, (part + 1) * lines_per_block)
        for f2 in range(cos_ref.shape[1] // blocks):
            picked = slice(f2 * lines_per_block, (f2 + 1) * lines_per_block)
            cos_ref[rows, f2 * blocks:(f2 + 1) * blocks] = x_re[picked] * norm_scale
            sin_ref[rows, f2 * blocks:(f2 + 1) * blocks] = x_neg_im[picked] * norm_scale


def line_spectra(x):
    blocks, width = x.shape
    lines = width // SUB
    f2_total = HALF // blocks
    tables = dft_tables(blocks, LANE // SUB, f2_total)
    out = jax.ShapeDtypeStruct((lines, HALF), F32)
    return pl.pallas_call(
        dft_kernel,
        out_shape=(out, out),
        cost_estimate=pl.CostEstimate(
            flops=2 * 3 * (2 * blocks * blocks * width + 4 * f2_total * width * blocks * LANE // SUB),
            bytes_accessed=4 * (blocks * width + 2 * lines * HALF + 2 * blocks * LANE) + 2 * 4 * blocks * blocks,
            transcendentals=0,
        ),
    )(x, *tables)


def body(velocity, new_owner, box_block, box_count, box_level):
    owners = lax.axis_size("own")
    groups = lax.axis_size("bulk")
    slot_total = velocity.shape[3]
    per_pair = slot_total // owners
    parcel_rows = owners * per_pair
    held_blocks = slot_total // 2
    first_block = lax.axis_index("bulk") * held_blocks
    slot_ids = jnp.arange(slot_total, dtype=jnp.int32)
    destination = new_owner[0, 0]
    filled = slot_ids < box_count[0, 0]
    owner_hits = (
        filled[:, None] & (destination[:, None] == jnp.arange(owners, dtype=jnp.int32)[None, :])
    ).astype(jnp.int32)
    earlier = jnp.cumsum(owner_hits, axis=0) - owner_hits
    order_rank = jnp.sum(earlier * owner_hits, axis=1)
    position = jnp.where(filled, destination * per_pair + order_rank, parcel_rows)
    parcel_ids = jnp.arange(parcel_rows, dtype=jnp.int32)
    factor = level_factor(box_level[0, 0])
    permute = jnp.where(position[None, :] == parcel_ids[:, None], factor[None, :], 0.0).astype(BF16)
    source = jnp.full((parcel_rows,), slot_total, jnp.int32).at[position].set(slot_ids, mode="drop")
    occupied = source < slot_total
    source_safe = jnp.minimum(source, slot_total - 1)
    blocks_out = jnp.where(occupied, jnp.take(box_block[0, 0], source_safe), -1).astype(F32)
    codes = jnp.broadcast_to(blocks_out[:, None], (parcel_rows, CODE_W))

    cells = velocity[:, 0, 0]
    flat = jnp.pad(cells, ((0, 0), (0, 0), (0, ROW_PAD - cells.shape[-1])))
    parcel = source_divergence(flat, permute, codes)

    arrived = lax.all_to_all(parcel, "own", split_axis=0, concat_axis=0, tiled=True)
    code_in = arrived[:, BOX * FACE]
    place_at = jnp.where(code_in >= 0, code_in.astype(jnp.int32) - first_block, held_blocks)
    chosen = jnp.zeros((held_blocks,), jnp.int32).at[place_at].set(parcel_ids, mode="drop")
    rows_per_group = BOX * FACE // groups
    column = arrived[:, : BOX * FACE].reshape(parcel_rows, groups, rows_per_group)
    outgoing = jnp.transpose(jnp.take(column, chosen, axis=0), (1, 0, 2))
    gathered = lax.all_to_all(outgoing, "bulk", split_axis=0, concat_axis=0, tiled=True)
    cosine, sine_vals = line_spectra(gathered.reshape(groups * held_blocks, rows_per_group))
    return (cosine[None], sine_vals[None])


def solution(mesh):
    in_specs = (
        P(None, "bulk", "own", None, None),
        P("bulk", "own", None),
        P("bulk", "own", None),
        P("bulk", "own"),
        P("bulk", "own", None),
    )
    out_specs = (P("own", "bulk", None), P("own", "bulk", None))
    return jax.shard_map(body, mesh=mesh, in_specs=in_specs, out_specs=out_specs, check_vma=False)
```

```python
import math

import ml_dtypes
import numpy as np

import jax
import jax.numpy as jnp
from jax import lax
from jax.experimental import pallas as pl
from jax.experimental.pallas import tpu as pltpu
from jax.sharding import PartitionSpec as P

BOX = 16
GHOST = BOX + 2
PLANE = GHOST * GHOST
PLANE_PAD = 384
FACE = BOX * BOX
HALF = 3072
NX = 6144
SUB = 16
CODE_W = 128

HIGHEST = lax.Precision.HIGHEST
F32 = jnp.float32
BF16 = jnp.bfloat16


def level_factor(level):
    return jnp.where(level == 1, 0.5, jnp.where(level == 2, 1.0, 2.0)).astype(jnp.float32)


def selection_table():
    sel = np.zeros((PLANE_PAD, FACE), np.float32)
    for j in range(BOX):
        for k in range(BOX):
            sel[GHOST * (j + 1) + k + 1, j * BOX + k] = 1.0
    return jnp.asarray(sel, BF16)


def _split2(x):
    hi = x.astype(BF16)
    lo = (x - hi.astype(F32)).astype(BF16)
    return hi, lo


def _split3(x):
    hi = x.astype(BF16)
    rest = x - hi.astype(F32)
    mid = rest.astype(BF16)
    lo = (rest - mid.astype(F32)).astype(BF16)
    return hi, mid, lo


def _dot(a, b):
    return jnp.dot(a, b, preferred_element_type=F32)


def _exact_right(x, m):
    hi, mid, lo = _split3(x)
    return _dot(hi, m) + _dot(mid, m) + _dot(lo, m)


def _exact_left(m, x):
    hi, mid, lo = _split3(x)
    return _dot(m, hi) + _dot(m, mid) + _dot(m, lo)


WINDOW = 512
ROW_PAD = 6016


def _plane(x_ref, field, p):
    start = PLANE * p
    base = (start // 128) * 128
    off = start - base
    w = x_ref[field, :, base:base + WINDOW]
    if off:
        w = pltpu.roll(w, WINDOW - off, 1)
    return w[:, :PLANE_PAD]


def divergence_kernel(x_ref, sel_ref, p_ref, code_ref, o_ref):
    h = pl.program_id(0)
    pieces = []
    for i in range(BOX):
        u = _plane(x_ref, 0, i + 1)
        w = _plane(x_ref, 2, i + 1)
        along_x = pltpu.roll(u, PLANE_PAD - 1, 1) - pltpu.roll(u, 1, 1)
        along_y = _plane(x_ref, 1, i + 2) - _plane(x_ref, 1, i)
        along_z = pltpu.roll(w, PLANE_PAD - GHOST, 1) - pltpu.roll(w, GHOST, 1)
        pieces.append(along_x + (along_y + along_z))
    interior = _exact_right(jnp.concatenate(pieces, axis=0), sel_ref[...])
    rows = p_ref.shape[2]
    permute = p_ref[0]
    chunk_rows = o_ref.shape[0]
    data_w = o_ref.shape[1] - code_ref.shape[1]
    owners = code_ref.shape[0]
    per_pair = permute.shape[0] // owners
    groups = chunk_rows // owners
    planes_per_group = BOX // groups
    piece_w = data_w // per_pair

    @pl.when(h == 0)
    def _():
        o_ref[...] = jnp.zeros_like(o_ref)
        for g in range(groups):
            o_ref[g * owners:(g + 1) * owners, data_w:] = code_ref[...]

    for i in range(BOX):
        moved = _exact_left(permute, interior[i * rows:(i + 1) * rows])
        g, half = divmod(i, planes_per_group)
        for t in range(per_pair):
            lane0 = t * piece_w + half * FACE
            o_ref[g * owners:(g + 1) * owners, lane0:lane0 + FACE] += moved[t * owners:(t + 1) * owners]


def source_divergence(flat, permute, codes, groups, halves=2):
    slots = flat.shape[1]
    part = slots // halves
    owners = codes.shape[0]
    out_w = BOX * FACE // groups * (slots // owners) + CODE_W
    sel = selection_table()
    return pl.pallas_call(
        divergence_kernel,
        grid=(halves,),
        in_specs=[
            pl.BlockSpec((3, part, ROW_PAD), lambda h: (0, h, 0)),
            pl.BlockSpec((PLANE_PAD, FACE), lambda h: (0, 0)),
            pl.BlockSpec((1, slots, part), lambda h: (h, 0, 0)),
            pl.BlockSpec((owners, CODE_W), lambda h: (0, 0)),
        ],
        out_specs=pl.BlockSpec((groups * owners, out_w), lambda h: (0, 0)),
        out_shape=jax.ShapeDtypeStruct((groups * owners, out_w), F32),
        cost_estimate=pl.CostEstimate(
            flops=2 * slots * BOX * PLANE_PAD * FACE * 3 + 2 * slots * slots * BOX * FACE * 3,
            bytes_accessed=4 * (3 * slots * ROW_PAD + groups * owners * out_w),
            transcendentals=0,
        ),
    )(flat, sel, jnp.transpose(permute.reshape(slots, halves, part), (1, 0, 2)), codes)


def _split_np(t):
    hi = t.astype(ml_dtypes.bfloat16)
    lo = (t - hi.astype(np.float64)).astype(ml_dtypes.bfloat16)
    return jnp.asarray(hi), jnp.asarray(lo)


def _angles(product, period):
    return (2.0 * np.pi / period) * (product % period).astype(np.float64)


def dft_tables(blocks, lines_per_block, f2_total):
    g_ids = np.arange(blocks, dtype=np.int64)
    stage_one = _angles(g_ids[:, None] * g_ids[None, :], blocks)
    lanes = lines_per_block * SUB
    twist = _angles(g_ids[:, None] * (np.arange(lanes) % SUB)[None, :], NX)
    row = np.arange(f2_total * lines_per_block)
    col = np.arange(lanes)
    same_line = (row[:, None] % lines_per_block) == (col[None, :] // SUB)
    last = _angles((row[:, None] // lines_per_block) * (col[None, :] % SUB), SUB)
    return (
        *_split_np(np.cos(stage_one)),
        *_split_np(np.sin(stage_one)),
        jnp.asarray(np.cos(twist), F32),
        jnp.asarray(np.sin(twist), F32),
        *_split_np(np.where(same_line, np.cos(last), 0.0)),
        *_split_np(np.where(same_line, np.sin(last), 0.0)),
    )


def _mm3(a_hi, a_lo, b_hi, b_lo, dims=None):
    if dims is None:
        f = _dot
    else:
        f = lambda a, b: lax.dot_general(a, b, dims, preferred_element_type=F32)
    return f(a_hi, b_hi) + (f(a_hi, b_lo) + f(a_lo, b_hi))


NT = (((1,), (1,)), ((), ()))
LANE = 128


def dft_kernel(x_ref, c1h, c1l, s1h, s1l, twc_ref, tws_ref, bch, bcl, bsh, bsl, cos_ref, sin_ref):
    xh, xl = _split2(x_ref[...])
    y_re = _mm3(c1h[...], c1l[...], xh, xl)
    y_im = -_mm3(s1h[...], s1l[...], xh, xl)
    twc = twc_ref[...]
    tws = tws_ref[...]
    bc_h, bc_l, bs_h, bs_l = bch[...], bcl[...], bsh[...], bsl[...]
    norm_scale = 1.0 / math.sqrt(NX)
    blocks = x_ref.shape[0]
    lines_per_block = LANE // SUB
    for part in range(x_ref.shape[1] // LANE):
        cols = slice(part * LANE, (part + 1) * LANE)
        yr = y_re[:, cols]
        yi = y_im[:, cols]
        zrh, zrl = _split2(yr * twc + yi * tws)
        zih, zil = _split2(yi * twc - yr * tws)
        x_re = _mm3(bc_h, bc_l, zrh, zrl, NT) + _mm3(bs_h, bs_l, zih, zil, NT)
        x_neg_im = _mm3(bs_h, bs_l, zrh, zrl, NT) - _mm3(bc_h, bc_l, zih, zil, NT)
        rows = slice(part * lines_per_block, (part + 1) * lines_per_block)
        for f2 in range(cos_ref.shape[1] // blocks):
            picked = slice(f2 * lines_per_block, (f2 + 1) * lines_per_block)
            cos_ref[rows, f2 * blocks:(f2 + 1) * blocks] = x_re[picked] * norm_scale
            sin_ref[rows, f2 * blocks:(f2 + 1) * blocks] = x_neg_im[picked] * norm_scale


def line_spectra(x):
    blocks, width = x.shape
    lines = width // SUB
    f2_total = HALF // blocks
    tables = dft_tables(blocks, LANE // SUB, f2_total)
    out = jax.ShapeDtypeStruct((lines, HALF), F32)
    return pl.pallas_call(
        dft_kernel,
        out_shape=(out, out),
        cost_estimate=pl.CostEstimate(
            flops=2 * 3 * (2 * blocks * blocks * width + 4 * f2_total * width * blocks * LANE // SUB),
            bytes_accessed=4 * (blocks * width + 2 * lines * HALF + 2 * blocks * LANE) + 2 * 4 * blocks * blocks,
            transcendentals=0,
        ),
    )(x, *tables)


def body(velocity, new_owner, box_block, box_count, box_level):
    owners = lax.axis_size("own")
    groups = lax.axis_size("bulk")
    slot_total = velocity.shape[3]
    per_pair = slot_total // owners
    parcel_rows = owners * per_pair
    held_blocks = slot_total // 2
    first_block = lax.axis_index("bulk") * held_blocks
    slot_ids = jnp.arange(slot_total, dtype=jnp.int32)
    destination = new_owner[0, 0]
    filled = slot_ids < box_count[0, 0]
    owner_hits = (
        filled[:, None] & (destination[:, None] == jnp.arange(owners, dtype=jnp.int32)[None, :])
    ).astype(jnp.int32)
    earlier = jnp.cumsum(owner_hits, axis=0) - owner_hits
    order_rank = jnp.sum(earlier * owner_hits, axis=1)
    position = jnp.where(filled, destination * per_pair + order_rank, parcel_rows)
    parcel_ids = jnp.arange(parcel_rows, dtype=jnp.int32)
    factor = level_factor(box_level[0, 0])
    row_of = jnp.where(filled, order_rank * owners + destination, parcel_rows)
    permute = jnp.where(row_of[None, :] == parcel_ids[:, None], factor[None, :], 0.0).astype(BF16)
    source = jnp.full((parcel_rows,), slot_total, jnp.int32).at[position].set(slot_ids, mode="drop")
    occupied = source < slot_total
    source_safe = jnp.minimum(source, slot_total - 1)
    blocks_out = jnp.where(occupied, jnp.take(box_block[0, 0], source_safe), -1).astype(F32)
    code_lanes = jnp.arange(CODE_W, dtype=jnp.int32)
    codes = jnp.where(
        code_lanes[None, :] < per_pair,
        jnp.take(blocks_out.reshape(owners, per_pair), jnp.minimum(code_lanes, per_pair - 1), axis=1),
        0.0,
    )

    cells = velocity[:, 0, 0]
    flat = jnp.pad(cells, ((0, 0), (0, 0), (0, ROW_PAD - cells.shape[-1])))
    parcel = source_divergence(flat, permute, codes, groups)

    arrived = lax.all_to_all(parcel, ("bulk", "own"), split_axis=0, concat_axis=0, tiled=True)
    piece_w = BOX * FACE // groups
    data_w = piece_w * per_pair
    code_in = arrived[:, data_w:data_w + per_pair].reshape(-1)
    total_blocks = groups * held_blocks
    place_at = jnp.where(code_in >= 0, code_in.astype(jnp.int32), total_blocks)
    arrived_ids = jnp.arange(code_in.shape[0], dtype=jnp.int32)
    chosen = jnp.zeros((total_blocks,), jnp.int32).at[place_at].set(arrived_ids, mode="drop")
    pieces = arrived[:, :data_w].reshape(-1, piece_w)
    cosine, sine_vals = line_spectra(jnp.take(pieces, chosen, axis=0))
    return (cosine[None], sine_vals[None])


def solution(mesh):
    in_specs = (
        P(None, "bulk", "own", None, None),
        P("bulk", "own", None),
        P("bulk", "own", None),
        P("bulk", "own"),
        P("bulk", "own", None),
    )
    out_specs = (P("own", "bulk", None), P("own", "bulk", None))
    return jax.shard_map(body, mesh=mesh, in_specs=in_specs, out_specs=out_specs, check_vma=False)
```

```python
import math

import ml_dtypes
import numpy as np

import jax
import jax.numpy as jnp
from jax import lax
from jax.experimental import pallas as pl
from jax.experimental.pallas import tpu as pltpu
from jax.sharding import PartitionSpec as P

BOX = 16
GHOST = BOX + 2
PLANE = GHOST * GHOST
PLANE_PAD = 384
FACE = BOX * BOX
HALF = 3072
NX = 6144
SUB = 16
CODE_W = 128

HIGHEST = lax.Precision.HIGHEST
F32 = jnp.float32
BF16 = jnp.bfloat16


def level_factor(level):
    return jnp.where(level == 1, 0.5, jnp.where(level == 2, 1.0, 2.0)).astype(jnp.float32)


def selection_table():
    sel = np.zeros((PLANE_PAD, FACE), np.float32)
    for j in range(BOX):
        for k in range(BOX):
            sel[GHOST * (j + 1) + k + 1, j * BOX + k] = 1.0
    return jnp.asarray(sel, BF16)


def _split2(x):
    hi = x.astype(BF16)
    lo = (x - hi.astype(F32)).astype(BF16)
    return hi, lo


def _split3(x):
    hi = x.astype(BF16)
    rest = x - hi.astype(F32)
    mid = rest.astype(BF16)
    lo = (rest - mid.astype(F32)).astype(BF16)
    return hi, mid, lo


def _dot(a, b):
    return jnp.dot(a, b, preferred_element_type=F32)


def _exact_right(x, m):
    hi, mid, lo = _split3(x)
    return _dot(hi, m) + _dot(mid, m) + _dot(lo, m)


def _exact_left(m, x):
    hi, mid, lo = _split3(x)
    return _dot(m, hi) + _dot(m, mid) + _dot(m, lo)


WINDOW = 512
ROW_PAD = 6016


def _plane(x_ref, field, p):
    start = PLANE * p
    base = (start // 128) * 128
    off = start - base
    w = x_ref[field, :, base:base + WINDOW]
    if off:
        w = pltpu.roll(w, WINDOW - off, 1)
    return w[:, :PLANE_PAD]


def divergence_kernel(src_ref, x_hbm, sel_ref, fac_ref, code_ref, o_ref, buf, sem):
    owners = code_ref.shape[0]
    per_pair = src_ref.shape[0] // owners
    chunk_rows = o_ref.shape[0]
    data_w = o_ref.shape[1] - code_ref.shape[1]
    groups = chunk_rows // owners
    planes_per_group = BOX // groups
    piece_w = data_w // per_pair

    def fetch(t, slot):
        for r in range(owners):
            pltpu.make_async_copy(
                x_hbm.at[:, pl.ds(src_ref[t * owners + r], 1), :],
                buf.at[slot, :, pl.ds(r, 1), :],
                sem.at[slot],
            ).start()

    def wait(slot):
        pltpu.make_async_copy(x_hbm.at[:, pl.ds(0, owners), :], buf.at[slot], sem.at[slot]).wait()

    fetch(0, 0)
    for g in range(groups):
        o_ref[g * owners:(g + 1) * owners, data_w:] = code_ref[...]
    sel = sel_ref[...]
    for t in range(per_pair):
        slot = t % 2
        if t + 1 < per_pair:
            fetch(t + 1, 1 - slot)
        wait(slot)
        x_ref = buf.at[slot]
        pieces = []
        for i in range(BOX):
            u = _plane(x_ref, 0, i + 1)
            w = _plane(x_ref, 2, i + 1)
            along_x = pltpu.roll(u, PLANE_PAD - 1, 1) - pltpu.roll(u, 1, 1)
            along_y = _plane(x_ref, 1, i + 2) - _plane(x_ref, 1, i)
            along_z = pltpu.roll(w, PLANE_PAD - GHOST, 1) - pltpu.roll(w, GHOST, 1)
            pieces.append(along_x + (along_y + along_z))
        interior = _exact_right(jnp.concatenate(pieces, axis=0), sel)
        fac = fac_ref[t * owners:(t + 1) * owners, :]
        for i in range(BOX):
            g, half = divmod(i, planes_per_group)
            lane0 = t * piece_w + half * FACE
            o_ref[g * owners:(g + 1) * owners, lane0:lane0 + FACE] = interior[i * owners:(i + 1) * owners] * fac


def source_divergence(flat, source, factor, codes, groups):
    slots = flat.shape[1]
    owners = codes.shape[0]
    out_w = BOX * FACE // groups * (slots // owners) + CODE_W
    sel = selection_table()
    vmem = pl.BlockSpec(memory_space=pltpu.VMEM)
    return pl.pallas_call(
        divergence_kernel,
        in_specs=[
            pl.BlockSpec(memory_space=pltpu.SMEM),
            pl.BlockSpec(memory_space=pl.ANY),
            vmem,
            vmem,
            vmem,
        ],
        out_specs=vmem,
        out_shape=jax.ShapeDtypeStruct((groups * owners, out_w), F32),
        scratch_shapes=[
            pltpu.VMEM((2, 3, owners, flat.shape[2]), F32),
            pltpu.SemaphoreType.DMA((2,)),
        ],
        cost_estimate=pl.CostEstimate(
            flops=2 * slots * BOX * PLANE_PAD * FACE * 3,
            bytes_accessed=4 * (3 * slots * ROW_PAD + groups * owners * out_w),
            transcendentals=0,
        ),
    )(source, flat, sel, jnp.broadcast_to(factor[:, None], (slots, FACE)), codes)


def _split_np(t):
    hi = t.astype(ml_dtypes.bfloat16)
    lo = (t - hi.astype(np.float64)).astype(ml_dtypes.bfloat16)
    return jnp.asarray(hi), jnp.asarray(lo)


def _angles(product, period):
    return (2.0 * np.pi / period) * (product % period).astype(np.float64)


def dft_tables(blocks, lines_per_block, f2_total):
    g_ids = np.arange(blocks, dtype=np.int64)
    stage_one = _angles(g_ids[:, None] * g_ids[None, :], blocks)
    lanes = lines_per_block * SUB
    twist = _angles(g_ids[:, None] * (np.arange(lanes) % SUB)[None, :], NX)
    row = np.arange(f2_total * lines_per_block)
    col = np.arange(lanes)
    same_line = (row[:, None] % lines_per_block) == (col[None, :] // SUB)
    last = _angles((row[:, None] // lines_per_block) * (col[None, :] % SUB), SUB)
    return (
        *_split_np(np.cos(stage_one)),
        *_split_np(np.sin(stage_one)),
        jnp.asarray(np.cos(twist), F32),
        jnp.asarray(np.sin(twist), F32),
        *_split_np(np.where(same_line, np.cos(last), 0.0)),
        *_split_np(np.where(same_line, np.sin(last), 0.0)),
    )


def _mm3(a_hi, a_lo, b_hi, b_lo, dims=None):
    if dims is None:
        f = _dot
    else:
        f = lambda a, b: lax.dot_general(a, b, dims, preferred_element_type=F32)
    return f(a_hi, b_hi) + (f(a_hi, b_lo) + f(a_lo, b_hi))


NT = (((1,), (1,)), ((), ()))
LANE = 128


def dft_kernel(x_ref, c1h, c1l, s1h, s1l, twc_ref, tws_ref, bch, bcl, bsh, bsl, cos_ref, sin_ref):
    xh, xl = _split2(x_ref[...])
    y_re = _mm3(c1h[...], c1l[...], xh, xl)
    y_im = -_mm3(s1h[...], s1l[...], xh, xl)
    twc = twc_ref[...]
    tws = tws_ref[...]
    bc_h, bc_l, bs_h, bs_l = bch[...], bcl[...], bsh[...], bsl[...]
    norm_scale = 1.0 / math.sqrt(NX)
    blocks = x_ref.shape[0]
    lines_per_block = LANE // SUB
    for part in range(x_ref.shape[1] // LANE):
        cols = slice(part * LANE, (part + 1) * LANE)
        yr = y_re[:, cols]
        yi = y_im[:, cols]
        zrh, zrl = _split2(yr * twc + yi * tws)
        zih, zil = _split2(yi * twc - yr * tws)
        x_re = _mm3(bc_h, bc_l, zrh, zrl, NT) + _mm3(bs_h, bs_l, zih, zil, NT)
        x_neg_im = _mm3(bs_h, bs_l, zrh, zrl, NT) - _mm3(bc_h, bc_l, zih, zil, NT)
        rows = slice(part * lines_per_block, (part + 1) * lines_per_block)
        for f2 in range(cos_ref.shape[1] // blocks):
            picked = slice(f2 * lines_per_block, (f2 + 1) * lines_per_block)
            cos_ref[rows, f2 * blocks:(f2 + 1) * blocks] = x_re[picked] * norm_scale
            sin_ref[rows, f2 * blocks:(f2 + 1) * blocks] = x_neg_im[picked] * norm_scale


def line_spectra(x):
    blocks, width = x.shape
    lines = width // SUB
    f2_total = HALF // blocks
    tables = dft_tables(blocks, LANE // SUB, f2_total)
    out = jax.ShapeDtypeStruct((lines, HALF), F32)
    return pl.pallas_call(
        dft_kernel,
        out_shape=(out, out),
        cost_estimate=pl.CostEstimate(
            flops=2 * 3 * (2 * blocks * blocks * width + 4 * f2_total * width * blocks * LANE // SUB),
            bytes_accessed=4 * (blocks * width + 2 * lines * HALF + 2 * blocks * LANE) + 2 * 4 * blocks * blocks,
            transcendentals=0,
        ),
    )(x, *tables)


def body(velocity, new_owner, box_block, box_count, box_level):
    owners = lax.axis_size("own")
    groups = lax.axis_size("bulk")
    slot_total = velocity.shape[3]
    per_pair = slot_total // owners
    parcel_rows = owners * per_pair
    held_blocks = slot_total // 2
    first_block = lax.axis_index("bulk") * held_blocks
    slot_ids = jnp.arange(slot_total, dtype=jnp.int32)
    destination = new_owner[0, 0]
    filled = slot_ids < box_count[0, 0]
    owner_hits = (
        filled[:, None] & (destination[:, None] == jnp.arange(owners, dtype=jnp.int32)[None, :])
    ).astype(jnp.int32)
    earlier = jnp.cumsum(owner_hits, axis=0) - owner_hits
    order_rank = jnp.sum(earlier * owner_hits, axis=1)
    position = jnp.where(filled, destination * per_pair + order_rank, parcel_rows)
    parcel_ids = jnp.arange(parcel_rows, dtype=jnp.int32)
    factor = level_factor(box_level[0, 0])
    source = jnp.full((parcel_rows,), slot_total, jnp.int32).at[position].set(slot_ids, mode="drop")
    occupied = source < slot_total
    source_safe = jnp.minimum(source, slot_total - 1)
    blocks_out = jnp.where(occupied, jnp.take(box_block[0, 0], source_safe), -1).astype(F32)
    code_lanes = jnp.arange(CODE_W, dtype=jnp.int32)
    codes = jnp.where(
        code_lanes[None, :] < per_pair,
        jnp.take(blocks_out.reshape(owners, per_pair), jnp.minimum(code_lanes, per_pair - 1), axis=1),
        0.0,
    )
    row_factor = jnp.where(occupied, jnp.take(factor, source_safe), 0.0)
    by_rank = lambda v: v.reshape(owners, per_pair).T.reshape(-1)

    cells = velocity[:, 0, 0]
    flat = jnp.pad(cells, ((0, 0), (0, 0), (0, ROW_PAD - cells.shape[-1])))
    parcel = source_divergence(flat, by_rank(source_safe), by_rank(row_factor), codes, groups)

    arrived = lax.all_to_all(parcel, ("bulk", "own"), split_axis=0, concat_axis=0, tiled=True)
    piece_w = BOX * FACE // groups
    data_w = piece_w * per_pair
    code_in = arrived[:, data_w:data_w + per_pair].reshape(-1)
    total_blocks = groups * held_blocks
    place_at = jnp.where(code_in >= 0, code_in.astype(jnp.int32), total_blocks)
    arrived_ids = jnp.arange(code_in.shape[0], dtype=jnp.int32)
    chosen = jnp.zeros((total_blocks,), jnp.int32).at[place_at].set(arrived_ids, mode="drop")
    pieces = arrived[:, :data_w].reshape(-1, piece_w)
    cosine, sine_vals = line_spectra(jnp.take(pieces, chosen, axis=0))
    return (cosine[None], sine_vals[None])


def solution(mesh):
    in_specs = (
        P(None, "bulk", "own", None, None),
        P("bulk", "own", None),
        P("bulk", "own", None),
        P("bulk", "own"),
        P("bulk", "own", None),
    )
    out_specs = (P("own", "bulk", None), P("own", "bulk", None))
    return jax.shard_map(body, mesh=mesh, in_specs=in_specs, out_specs=out_specs, check_vma=False)
```

```python
import math

import ml_dtypes
import numpy as np

import jax
import jax.numpy as jnp
from jax import lax
from jax.experimental import pallas as pl
from jax.experimental.pallas import tpu as pltpu
from jax.sharding import PartitionSpec as P

BOX = 16
GHOST = BOX + 2
PLANE = GHOST * GHOST
PLANE_PAD = 384
FACE = BOX * BOX
HALF = 3072
NX = 6144
SUB = 16
CODE_W = 128

HIGHEST = lax.Precision.HIGHEST
F32 = jnp.float32
BF16 = jnp.bfloat16


def level_factor(level):
    return jnp.where(level == 1, 0.5, jnp.where(level == 2, 1.0, 2.0)).astype(jnp.float32)


def selection_table():
    sel = np.zeros((PLANE_PAD, FACE), np.float32)
    for j in range(BOX):
        for k in range(BOX):
            sel[GHOST * (j + 1) + k + 1, j * BOX + k] = 1.0
    return jnp.asarray(sel, BF16)


def _split2(x):
    hi = x.astype(BF16)
    lo = (x - hi.astype(F32)).astype(BF16)
    return hi, lo


def _split3(x):
    hi = x.astype(BF16)
    rest = x - hi.astype(F32)
    mid = rest.astype(BF16)
    lo = (rest - mid.astype(F32)).astype(BF16)
    return hi, mid, lo


def _dot(a, b):
    return jnp.dot(a, b, preferred_element_type=F32)


def _exact_right(x, m):
    hi, mid, lo = _split3(x)
    return _dot(hi, m) + _dot(mid, m) + _dot(lo, m)


def _exact_left(m, x):
    hi, mid, lo = _split3(x)
    return _dot(m, hi) + _dot(m, mid) + _dot(m, lo)


WINDOW = 512
ROW_PAD = 6016


def _plane(x_ref, field, p):
    start = PLANE * p
    base = (start // 128) * 128
    off = start - base
    w = x_ref[field, :, base:base + WINDOW]
    if off:
        w = pltpu.roll(w, WINDOW - off, 1)
    return w[:, :PLANE_PAD]


def divergence_kernel(src_ref, x_hbm, sel_ref, fac_ref, code_ref, o_ref, buf, sem):
    owners = src_ref.shape[0]
    chunk_rows = o_ref.shape[0]
    groups = chunk_rows // owners
    planes_per_group = BOX // groups
    for r in range(owners):
        pltpu.make_async_copy(
            x_hbm.at[:, pl.ds(src_ref[r], 1), :], buf.at[:, pl.ds(r, 1), :], sem.at[0]
        ).start()
    data_w = o_ref.shape[1] - code_ref.shape[1]
    for g in range(groups):
        o_ref[g * owners:(g + 1) * owners, data_w:] = code_ref[...]
    sel = sel_ref[...]
    pltpu.make_async_copy(x_hbm.at[:, pl.ds(0, owners), :], buf, sem.at[0]).wait()
    pieces = []
    for i in range(BOX):
        u = _plane(buf, 0, i + 1)
        w = _plane(buf, 2, i + 1)
        along_x = pltpu.roll(u, PLANE_PAD - 1, 1) - pltpu.roll(u, 1, 1)
        along_y = _plane(buf, 1, i + 2) - _plane(buf, 1, i)
        along_z = pltpu.roll(w, PLANE_PAD - GHOST, 1) - pltpu.roll(w, GHOST, 1)
        pieces.append(along_x + (along_y + along_z))
    interior = _exact_right(jnp.concatenate(pieces, axis=0), sel)
    fac = fac_ref[...]
    for i in range(BOX):
        g, half = divmod(i, planes_per_group)
        o_ref[g * owners:(g + 1) * owners, half * FACE:(half + 1) * FACE] = interior[i * owners:(i + 1) * owners] * fac


def source_divergence(flat, source, factor, codes, groups):
    owners = source.shape[0]
    out_w = BOX * FACE // groups + CODE_W
    sel = selection_table()
    vmem = pl.BlockSpec(memory_space=pltpu.VMEM)
    operands = [source, flat, sel, jnp.broadcast_to(factor[:, None], (owners, FACE)), codes]
    return pl.pallas_call(
        divergence_kernel,
        in_specs=[pl.BlockSpec(memory_space=pltpu.SMEM), pl.BlockSpec(memory_space=pl.ANY)]
        + [vmem] * (len(operands) - 2),
        out_specs=vmem,
        out_shape=jax.ShapeDtypeStruct((groups * owners, out_w), F32),
        scratch_shapes=[
            pltpu.VMEM((3, owners, flat.shape[2]), F32),
            pltpu.SemaphoreType.DMA((1,)),
        ],
        cost_estimate=pl.CostEstimate(
            flops=2 * owners * BOX * PLANE_PAD * FACE * 3,
            bytes_accessed=4 * (3 * owners * ROW_PAD + groups * owners * out_w),
            transcendentals=0,
        ),
    )(*operands)


def _split_np(t):
    hi = t.astype(ml_dtypes.bfloat16)
    lo = (t - hi.astype(np.float64)).astype(ml_dtypes.bfloat16)
    return jnp.asarray(hi), jnp.asarray(lo)


def _angles(product, period):
    return (2.0 * np.pi / period) * (product % period).astype(np.float64)


def dft_tables(blocks, lines_per_block, f2_total):
    g_ids = np.arange(blocks, dtype=np.int64)
    stage_one = _angles(g_ids[:, None] * g_ids[None, :], blocks)
    lanes = lines_per_block * SUB
    twist = _angles(g_ids[:, None] * (np.arange(lanes) % SUB)[None, :], NX)
    row = np.arange(f2_total * lines_per_block)
    col = np.arange(lanes)
    same_line = (row[:, None] % lines_per_block) == (col[None, :] // SUB)
    last = _angles((row[:, None] // lines_per_block) * (col[None, :] % SUB), SUB)
    return (
        *_split_np(np.cos(stage_one)),
        *_split_np(np.sin(stage_one)),
        jnp.asarray(np.cos(twist), F32),
        jnp.asarray(np.sin(twist), F32),
        *_split_np(np.where(same_line, np.cos(last), 0.0)),
        *_split_np(np.where(same_line, np.sin(last), 0.0)),
    )


def _mm3(a_hi, a_lo, b_hi, b_lo, dims=None):
    if dims is None:
        f = _dot
    else:
        f = lambda a, b: lax.dot_general(a, b, dims, preferred_element_type=F32)
    return f(a_hi, b_hi) + (f(a_hi, b_lo) + f(a_lo, b_hi))


NT = (((1,), (1,)), ((), ()))
LANE = 128


def dft_kernel(x_ref, c1h, c1l, s1h, s1l, twc_ref, tws_ref, bch, bcl, bsh, bsl, cos_ref, sin_ref):
    xh, xl = _split2(x_ref[...])
    y_re = _mm3(c1h[...], c1l[...], xh, xl)
    y_im = -_mm3(s1h[...], s1l[...], xh, xl)
    twc = twc_ref[...]
    tws = tws_ref[...]
    bc_h, bc_l, bs_h, bs_l = bch[...], bcl[...], bsh[...], bsl[...]
    norm_scale = 1.0 / math.sqrt(NX)
    blocks = x_ref.shape[0]
    lines_per_block = LANE // SUB
    for part in range(x_ref.shape[1] // LANE):
        cols = slice(part * LANE, (part + 1) * LANE)
        yr = y_re[:, cols]
        yi = y_im[:, cols]
        zrh, zrl = _split2(yr * twc + yi * tws)
        zih, zil = _split2(yi * twc - yr * tws)
        x_re = _mm3(bc_h, bc_l, zrh, zrl, NT) + _mm3(bs_h, bs_l, zih, zil, NT)
        x_neg_im = _mm3(bs_h, bs_l, zrh, zrl, NT) - _mm3(bc_h, bc_l, zih, zil, NT)
        rows = slice(part * lines_per_block, (part + 1) * lines_per_block)
        for f2 in range(cos_ref.shape[1] // blocks):
            picked = slice(f2 * lines_per_block, (f2 + 1) * lines_per_block)
            cos_ref[rows, f2 * blocks:(f2 + 1) * blocks] = x_re[picked] * norm_scale
            sin_ref[rows, f2 * blocks:(f2 + 1) * blocks] = x_neg_im[picked] * norm_scale


def line_spectra(x):
    blocks, width = x.shape
    lines = width // SUB
    f2_total = HALF // blocks
    tables = dft_tables(blocks, LANE // SUB, f2_total)
    out = jax.ShapeDtypeStruct((lines, HALF), F32)
    return pl.pallas_call(
        dft_kernel,
        out_shape=(out, out),
        cost_estimate=pl.CostEstimate(
            flops=2 * 3 * (2 * blocks * blocks * width + 4 * f2_total * width * blocks * LANE // SUB),
            bytes_accessed=4 * (blocks * width + 2 * lines * HALF + 2 * blocks * LANE) + 2 * 4 * blocks * blocks,
            transcendentals=0,
        ),
    )(x, *tables)


def body(velocity, new_owner, box_block, box_count, box_level):
    owners = lax.axis_size("own")
    groups = lax.axis_size("bulk")
    slot_total = velocity.shape[3]
    per_pair = slot_total // owners
    parcel_rows = owners * per_pair
    held_blocks = slot_total // 2
    first_block = lax.axis_index("bulk") * held_blocks
    slot_ids = jnp.arange(slot_total, dtype=jnp.int32)
    destination = new_owner[0, 0]
    filled = slot_ids < box_count[0, 0]
    owner_hits = (
        filled[:, None] & (destination[:, None] == jnp.arange(owners, dtype=jnp.int32)[None, :])
    ).astype(jnp.int32)
    earlier = jnp.cumsum(owner_hits, axis=0) - owner_hits
    order_rank = jnp.sum(earlier * owner_hits, axis=1)
    position = jnp.where(filled, destination * per_pair + order_rank, parcel_rows)
    parcel_ids = jnp.arange(parcel_rows, dtype=jnp.int32)
    factor = level_factor(box_level[0, 0])
    source = jnp.full((parcel_rows,), slot_total, jnp.int32).at[position].set(slot_ids, mode="drop")
    occupied = source < slot_total
    source_safe = jnp.minimum(source, slot_total - 1)
    blocks_out = jnp.where(occupied, jnp.take(box_block[0, 0], source_safe), -1).astype(F32)
    code_lanes = jnp.arange(CODE_W, dtype=jnp.int32)
    codes = jnp.where(
        code_lanes[None, :] < per_pair,
        jnp.take(blocks_out.reshape(owners, per_pair), jnp.minimum(code_lanes, per_pair - 1), axis=1),
        0.0,
    )
    row_factor = jnp.where(occupied, jnp.take(factor, source_safe), 0.0)

    cells = velocity[:, 0, 0]
    flat = jnp.pad(cells, ((0, 0), (0, 0), (0, ROW_PAD - cells.shape[-1])))
    by_rank = lambda v: v.reshape(owners, per_pair).T
    sources = by_rank(source_safe)
    factors = by_rank(row_factor)
    arrived = []
    for t in range(per_pair):
        parcel = source_divergence(flat, sources[t], factors[t], codes, groups)
        if t:
            parcel = parcel[:, :BOX * FACE // groups]
        arrived.append(lax.all_to_all(parcel, ("bulk", "own"), split_axis=0, concat_axis=0, tiled=True))
    piece_w = BOX * FACE // groups
    code_in = arrived[0][:, piece_w:piece_w + per_pair].T.reshape(-1)
    total_blocks = groups * held_blocks
    place_at = jnp.where(code_in >= 0, code_in.astype(jnp.int32), total_blocks)
    arrived_ids = jnp.arange(code_in.shape[0], dtype=jnp.int32)
    chosen = jnp.zeros((total_blocks,), jnp.int32).at[place_at].set(arrived_ids, mode="drop")
    pieces = jnp.concatenate([arrived[0][:, :piece_w]] + arrived[1:], axis=0)
    x = jnp.take(pieces, chosen, axis=0)
    cosine, sine_vals = line_spectra(x)
    return (cosine[None], sine_vals[None])


def solution(mesh):
    in_specs = (
        P(None, "bulk", "own", None, None),
        P("bulk", "own", None),
        P("bulk", "own", None),
        P("bulk", "own"),
        P("bulk", "own", None),
    )
    out_specs = (P("own", "bulk", None), P("own", "bulk", None))
    return jax.shard_map(body, mesh=mesh, in_specs=in_specs, out_specs=out_specs, check_vma=False)
```

```python
import math

import ml_dtypes
import numpy as np

import jax
import jax.numpy as jnp
from jax import lax
from jax.experimental import pallas as pl
from jax.experimental.pallas import tpu as pltpu
from jax.sharding import PartitionSpec as P

BOX = 16
GHOST = BOX + 2
PLANE = GHOST * GHOST
PLANE_PAD = 384
FACE = BOX * BOX
HALF = 3072
NX = 6144
SUB = 16
CODE_W = 128

HIGHEST = lax.Precision.HIGHEST
F32 = jnp.float32
BF16 = jnp.bfloat16


def level_factor(level):
    return jnp.where(level == 1, 0.5, jnp.where(level == 2, 1.0, 2.0)).astype(jnp.float32)


def selection_table():
    sel = np.zeros((PLANE_PAD, FACE), np.float32)
    for j in range(BOX):
        for k in range(BOX):
            sel[GHOST * (j + 1) + k + 1, j * BOX + k] = 1.0
    return jnp.asarray(sel, BF16)


def _split2(x):
    hi = x.astype(BF16)
    lo = (x - hi.astype(F32)).astype(BF16)
    return hi, lo


def _split3(x):
    hi = x.astype(BF16)
    rest = x - hi.astype(F32)
    mid = rest.astype(BF16)
    lo = (rest - mid.astype(F32)).astype(BF16)
    return hi, mid, lo


def _dot(a, b):
    return jnp.dot(a, b, preferred_element_type=F32)


def _exact_right(x, m):
    hi, mid, lo = _split3(x)
    return _dot(hi, m) + _dot(mid, m) + _dot(lo, m)


def _exact_left(m, x):
    hi, mid, lo = _split3(x)
    return _dot(m, hi) + _dot(m, mid) + _dot(m, lo)


WINDOW = 512
ROW_PAD = 6016


def _plane(x_ref, field, p):
    start = PLANE * p
    base = (start // 128) * 128
    off = start - base
    w = x_ref[field, :, base:base + WINDOW]
    if off:
        w = pltpu.roll(w, WINDOW - off, 1)
    return w[:, :PLANE_PAD]


def divergence_kernel(src_ref, x_hbm, sel_ref, fac_ref, code_ref, o_ref, buf, sem):
    owners = code_ref.shape[0]
    per_pair = src_ref.shape[0] // owners
    chunk_rows = o_ref.shape[0]
    data_w = o_ref.shape[1] - code_ref.shape[1]
    groups = chunk_rows // owners
    planes_per_group = BOX // groups
    piece_w = data_w // per_pair

    def fetch(t, slot):
        for r in range(owners):
            pltpu.make_async_copy(
                x_hbm.at[:, pl.ds(src_ref[t * owners + r], 1), :],
                buf.at[slot, :, pl.ds(r, 1), :],
                sem.at[slot],
            ).start()

    def wait(slot):
        pltpu.make_async_copy(x_hbm.at[:, pl.ds(0, owners), :], buf.at[slot], sem.at[slot]).wait()

    fetch(0, 0)
    for g in range(groups):
        o_ref[g * owners:(g + 1) * owners, data_w:] = code_ref[...]
    sel = sel_ref[...]
    for t in range(per_pair):
        slot = t % 2
        if t + 1 < per_pair:
            fetch(t + 1, 1 - slot)
        wait(slot)
        x_ref = buf.at[slot]
        pieces = []
        for i in range(BOX):
            u = _plane(x_ref, 0, i + 1)
            w = _plane(x_ref, 2, i + 1)
            along_x = pltpu.roll(u, PLANE_PAD - 1, 1) - pltpu.roll(u, 1, 1)
            along_y = _plane(x_ref, 1, i + 2) - _plane(x_ref, 1, i)
            along_z = pltpu.roll(w, PLANE_PAD - GHOST, 1) - pltpu.roll(w, GHOST, 1)
            pieces.append(along_x + (along_y + along_z))
        interior = _exact_right(jnp.concatenate(pieces, axis=0), sel)
        fac = fac_ref[t * owners:(t + 1) * owners, :]
        for i in range(BOX):
            g, half = divmod(i, planes_per_group)
            lane0 = t * piece_w + half * FACE
            o_ref[g * owners:(g + 1) * owners, lane0:lane0 + FACE] = interior[i * owners:(i + 1) * owners] * fac


def source_divergence(flat, source, factor, codes, groups):
    slots = flat.shape[1]
    owners = codes.shape[0]
    out_w = BOX * FACE // groups * (slots // owners) + CODE_W
    sel = selection_table()
    vmem = pl.BlockSpec(memory_space=pltpu.VMEM)
    return pl.pallas_call(
        divergence_kernel,
        in_specs=[
            pl.BlockSpec(memory_space=pltpu.SMEM),
            pl.BlockSpec(memory_space=pl.ANY),
            vmem,
            vmem,
            vmem,
        ],
        out_specs=vmem,
        out_shape=jax.ShapeDtypeStruct((groups * owners, out_w), F32),
        scratch_shapes=[
            pltpu.VMEM((2, 3, owners, flat.shape[2]), F32),
            pltpu.SemaphoreType.DMA((2,)),
        ],
        cost_estimate=pl.CostEstimate(
            flops=2 * slots * BOX * PLANE_PAD * FACE * 3,
            bytes_accessed=4 * (3 * slots * ROW_PAD + groups * owners * out_w),
            transcendentals=0,
        ),
    )(source, flat, sel, jnp.broadcast_to(factor[:, None], (slots, FACE)), codes)


def _split_np(t):
    hi = t.astype(ml_dtypes.bfloat16)
    lo = (t - hi.astype(np.float64)).astype(ml_dtypes.bfloat16)
    return jnp.asarray(hi), jnp.asarray(lo)


def _angles(product, period):
    return (2.0 * np.pi / period) * (product % period).astype(np.float64)


def dft_tables(blocks, lines_per_block, f2_total):
    g_ids = np.arange(blocks, dtype=np.int64)
    stage_one = _angles(g_ids[:, None] * g_ids[None, :], blocks)
    lanes = lines_per_block * SUB
    twist = _angles(g_ids[:, None] * (np.arange(lanes) % SUB)[None, :], NX)
    row = np.arange(f2_total * lines_per_block)
    col = np.arange(lanes)
    same_line = (row[:, None] % lines_per_block) == (col[None, :] // SUB)
    last = _angles((row[:, None] // lines_per_block) * (col[None, :] % SUB), SUB)
    return (
        *_split_np(np.cos(stage_one)),
        *_split_np(np.sin(stage_one)),
        jnp.asarray(np.cos(twist), F32),
        jnp.asarray(np.sin(twist), F32),
        *_split_np(np.where(same_line, np.cos(last), 0.0)),
        *_split_np(np.where(same_line, np.sin(last), 0.0)),
    )


def _mm3(a_hi, a_lo, b_hi, b_lo, dims=None):
    if dims is None:
        f = _dot
    else:
        f = lambda a, b: lax.dot_general(a, b, dims, preferred_element_type=F32)
    return f(a_hi, b_hi) + (f(a_hi, b_lo) + f(a_lo, b_hi))


NT = (((1,), (1,)), ((), ()))
LANE = 128


def dft_kernel(x_ref, c1h, c1l, s1h, s1l, twc_ref, tws_ref, bch, bcl, bsh, bsl, cos_ref, sin_ref):
    xh, xl = _split2(x_ref[...])
    y_re = _mm3(c1h[...], c1l[...], xh, xl)
    y_im = -_mm3(s1h[...], s1l[...], xh, xl)
    twc = twc_ref[...]
    tws = tws_ref[...]
    bc_h, bc_l, bs_h, bs_l = bch[...], bcl[...], bsh[...], bsl[...]
    norm_scale = 1.0 / math.sqrt(NX)
    blocks = x_ref.shape[0]
    lines_per_block = LANE // SUB
    for part in range(x_ref.shape[1] // LANE):
        cols = slice(part * LANE, (part + 1) * LANE)
        yr = y_re[:, cols]
        yi = y_im[:, cols]
        zrh, zrl = _split2(yr * twc + yi * tws)
        zih, zil = _split2(yi * twc - yr * tws)
        x_re = _mm3(bc_h, bc_l, zrh, zrl, NT) + _mm3(bs_h, bs_l, zih, zil, NT)
        x_neg_im = _mm3(bs_h, bs_l, zrh, zrl, NT) - _mm3(bc_h, bc_l, zih, zil, NT)
        rows = slice(part * lines_per_block, (part + 1) * lines_per_block)
        for f2 in range(cos_ref.shape[1] // blocks):
            picked = slice(f2 * lines_per_block, (f2 + 1) * lines_per_block)
            cos_ref[rows, f2 * blocks:(f2 + 1) * blocks] = x_re[picked] * norm_scale
            sin_ref[rows, f2 * blocks:(f2 + 1) * blocks] = x_neg_im[picked] * norm_scale


def line_spectra(x):
    blocks, width = x.shape
    lines = width // SUB
    f2_total = HALF // blocks
    tables = dft_tables(blocks, LANE // SUB, f2_total)
    out = jax.ShapeDtypeStruct((lines, HALF), F32)
    return pl.pallas_call(
        dft_kernel,
        out_shape=(out, out),
        cost_estimate=pl.CostEstimate(
            flops=2 * 3 * (2 * blocks * blocks * width + 4 * f2_total * width * blocks * LANE // SUB),
            bytes_accessed=4 * (blocks * width + 2 * lines * HALF + 2 * blocks * LANE) + 2 * 4 * blocks * blocks,
            transcendentals=0,
        ),
    )(x, *tables)


def body(velocity, new_owner, box_block, box_count, box_level):
    owners = lax.axis_size("own")
    groups = lax.axis_size("bulk")
    slot_total = velocity.shape[3]
    per_pair = slot_total // owners
    parcel_rows = owners * per_pair
    held_blocks = slot_total // 2
    first_block = lax.axis_index("bulk") * held_blocks
    slot_ids = jnp.arange(slot_total, dtype=jnp.int32)
    destination = new_owner[0, 0]
    filled = slot_ids < box_count[0, 0]
    same_owner = filled[:, None] & filled[None, :] & (destination[:, None] == destination[None, :])
    order_rank = jnp.sum((same_owner & (slot_ids[None, :] < slot_ids[:, None])).astype(jnp.int32), axis=1)
    row_of = jnp.where(filled, order_rank * owners + destination, parcel_rows)
    parcel_ids = jnp.arange(parcel_rows, dtype=jnp.int32)
    match = row_of[None, :] == parcel_ids[:, None]
    factor = level_factor(box_level[0, 0])
    source_safe = jnp.sum(jnp.where(match, slot_ids[None, :], 0), axis=1)
    row_factor = jnp.sum(jnp.where(match, factor[None, :], 0.0), axis=1)
    row_block = jnp.sum(jnp.where(match, box_block[0, 0][None, :] + 1, 0), axis=1) - 1
    code_lanes = jnp.arange(CODE_W, dtype=jnp.int32)
    by_owner = row_block.reshape(per_pair, owners).T
    codes = jnp.where(
        code_lanes[None, :] < per_pair,
        jnp.take(by_owner, jnp.minimum(code_lanes, per_pair - 1), axis=1),
        -1,
    ).astype(F32)

    cells = velocity[:, 0, 0]
    flat = jnp.pad(cells, ((0, 0), (0, 0), (0, ROW_PAD - cells.shape[-1])))
    parcel = source_divergence(flat, source_safe, row_factor, codes, groups)

    arrived = lax.all_to_all(parcel, ("bulk", "own"), split_axis=0, concat_axis=0, tiled=True)
    piece_w = BOX * FACE // groups
    data_w = piece_w * per_pair
    code_in = arrived[:, data_w:data_w + per_pair].reshape(-1)
    total_blocks = groups * held_blocks
    place_at = jnp.where(code_in >= 0, code_in.astype(jnp.int32), total_blocks)
    arrived_ids = jnp.arange(code_in.shape[0], dtype=jnp.int32)
    block_ids = jnp.arange(total_blocks, dtype=jnp.int32)
    chosen = jnp.sum(jnp.where(place_at[None, :] == block_ids[:, None], arrived_ids[None, :], 0), axis=1)
    pieces = arrived[:, :data_w].reshape(-1, piece_w)
    cosine, sine_vals = line_spectra(jnp.take(pieces, chosen, axis=0))
    return (cosine[None], sine_vals[None])


def solution(mesh):
    in_specs = (
        P(None, "bulk", "own", None, None),
        P("bulk", "own", None),
        P("bulk", "own", None),
        P("bulk", "own"),
        P("bulk", "own", None),
    )
    out_specs = (P("own", "bulk", None), P("own", "bulk", None))
    return jax.shard_map(body, mesh=mesh, in_specs=in_specs, out_specs=out_specs, check_vma=False)
```

```python
import math

import ml_dtypes
import numpy as np

import jax
import jax.numpy as jnp
from jax import lax
from jax.experimental import pallas as pl
from jax.experimental.pallas import tpu as pltpu
from jax.sharding import PartitionSpec as P

BOX = 16
GHOST = BOX + 2
PLANE = GHOST * GHOST
PLANE_PAD = 384
FACE = BOX * BOX
HALF = 3072
NX = 6144
SUB = 16
CODE_W = 128

HIGHEST = lax.Precision.HIGHEST
F32 = jnp.float32
BF16 = jnp.bfloat16


def level_factor(level):
    return jnp.where(level == 1, 0.5, jnp.where(level == 2, 1.0, 2.0)).astype(jnp.float32)


def selection_table():
    sel = np.zeros((PLANE_PAD, FACE), np.float32)
    for j in range(BOX):
        for k in range(BOX):
            sel[GHOST * (j + 1) + k + 1, j * BOX + k] = 1.0
    return jnp.asarray(sel, BF16)


def _split2(x):
    hi = x.astype(BF16)
    lo = (x - hi.astype(F32)).astype(BF16)
    return hi, lo


def _split3(x):
    hi = x.astype(BF16)
    rest = x - hi.astype(F32)
    mid = rest.astype(BF16)
    lo = (rest - mid.astype(F32)).astype(BF16)
    return hi, mid, lo


def _dot(a, b):
    return jnp.dot(a, b, preferred_element_type=F32)


def _exact_right(x, m):
    hi, mid, lo = _split3(x)
    return _dot(hi, m) + _dot(mid, m) + _dot(lo, m)


def _exact_left(m, x):
    hi, mid, lo = _split3(x)
    return _dot(m, hi) + _dot(m, mid) + _dot(m, lo)


WINDOW = 512
ROW_PAD = 6016


def _plane(x_ref, field, p):
    start = PLANE * p
    base = (start // 128) * 128
    off = start - base
    w = x_ref[field, :, base:base + WINDOW]
    if off:
        w = pltpu.roll(w, WINDOW - off, 1)
    return w[:, :PLANE_PAD]


def divergence_kernel(src_ref, x_hbm, v_hbm, sel_ref, fac_ref, code_ref, o_ref, buf_uw, buf_v, sem):
    owners = code_ref.shape[0]
    per_pair = src_ref.shape[0] // owners
    chunk_rows = o_ref.shape[0]
    data_w = o_ref.shape[1] - code_ref.shape[1]
    groups = chunk_rows // owners
    planes_per_group = BOX // groups
    piece_w = data_w // per_pair

    def fetch(t, slot):
        for r in range(owners):
            row = src_ref[t * owners + r]
            for k, field in enumerate((0, 2)):
                pltpu.make_async_copy(
                    x_hbm.at[field, pl.ds(row, 1), :], buf_uw.at[slot, k, pl.ds(r, 1), :], sem.at[slot, 0]
                ).start()
            pltpu.make_async_copy(
                v_hbm.at[pl.ds(row, 1), :], buf_v.at[slot, 0, pl.ds(r, 1), :], sem.at[slot, 1]
            ).start()

    def wait(slot):
        pltpu.make_async_copy(x_hbm.at[pl.ds(0, 2), pl.ds(0, owners), :], buf_uw.at[slot], sem.at[slot, 0]).wait()
        pltpu.make_async_copy(v_hbm.at[pl.ds(0, owners), :], buf_v.at[slot, 0], sem.at[slot, 1]).wait()

    fetch(0, 0)
    for g in range(groups):
        o_ref[g * owners:(g + 1) * owners, data_w:] = code_ref[...]
    sel = sel_ref[...]
    for t in range(per_pair):
        slot = t % 2
        if t + 1 < per_pair:
            fetch(t + 1, 1 - slot)
        wait(slot)
        uw_ref = buf_uw.at[slot]
        v_ref = buf_v.at[slot]
        v_planes = [_plane(v_ref, 0, p) for p in range(GHOST)]
        pieces = []
        for i in range(BOX):
            u = _plane(uw_ref, 0, i + 1)
            w = _plane(uw_ref, 1, i + 1)
            along_x = pltpu.roll(u, PLANE_PAD - 1, 1) - pltpu.roll(u, 1, 1)
            along_y = v_planes[i + 2] - v_planes[i]
            along_z = pltpu.roll(w, PLANE_PAD - GHOST, 1) - pltpu.roll(w, GHOST, 1)
            pieces.append(along_x + (along_y + along_z))
        interior = _exact_right(jnp.concatenate(pieces, axis=0), sel)
        fac = fac_ref[t * owners:(t + 1) * owners, :]
        for i in range(BOX):
            g, half = divmod(i, planes_per_group)
            lane0 = t * piece_w + half * FACE
            o_ref[g * owners:(g + 1) * owners, lane0:lane0 + FACE] = interior[i * owners:(i + 1) * owners] * fac


def source_divergence(cells, source, factor, codes, groups):
    slots = cells.shape[1]
    owners = codes.shape[0]
    out_w = BOX * FACE // groups * (slots // owners) + CODE_W
    sel = selection_table()
    spanwise = jnp.pad(cells[1], ((0, 0), (0, ROW_PAD - cells.shape[-1])))
    vmem = pl.BlockSpec(memory_space=pltpu.VMEM)
    return pl.pallas_call(
        divergence_kernel,
        in_specs=[
            pl.BlockSpec(memory_space=pltpu.SMEM),
            pl.BlockSpec(memory_space=pl.ANY),
            pl.BlockSpec(memory_space=pl.ANY),
            vmem,
            vmem,
            vmem,
        ],
        out_specs=vmem,
        out_shape=jax.ShapeDtypeStruct((groups * owners, out_w), F32),
        scratch_shapes=[
            pltpu.VMEM((2, 2, owners, cells.shape[2]), F32),
            pltpu.VMEM((2, 1, owners, ROW_PAD), F32),
            pltpu.SemaphoreType.DMA((2, 2)),
        ],
        cost_estimate=pl.CostEstimate(
            flops=2 * slots * BOX * PLANE_PAD * FACE * 3,
            bytes_accessed=4 * (3 * slots * ROW_PAD + groups * owners * out_w),
            transcendentals=0,
        ),
    )(source, cells, spanwise, sel, jnp.broadcast_to(factor[:, None], (slots, FACE)), codes)


def _split_np(t):
    hi = t.astype(ml_dtypes.bfloat16)
    lo = (t - hi.astype(np.float64)).astype(ml_dtypes.bfloat16)
    return jnp.asarray(hi), jnp.asarray(lo)


def _angles(product, period):
    return (2.0 * np.pi / period) * (product % period).astype(np.float64)


def dft_tables(blocks, lines_per_block, f2_total):
    g_ids = np.arange(blocks, dtype=np.int64)
    stage_one = _angles(g_ids[:, None] * g_ids[None, :], blocks)
    lanes = lines_per_block * SUB
    twist = _angles(g_ids[:, None] * (np.arange(lanes) % SUB)[None, :], NX)
    row = np.arange(f2_total * lines_per_block)
    col = np.arange(lanes)
    same_line = (row[:, None] % lines_per_block) == (col[None, :] // SUB)
    last = _angles((row[:, None] // lines_per_block) * (col[None, :] % SUB), SUB)
    return (
        *_split_np(np.cos(stage_one)),
        *_split_np(np.sin(stage_one)),
        jnp.asarray(np.cos(twist), F32),
        jnp.asarray(np.sin(twist), F32),
        *_split_np(np.where(same_line, np.cos(last), 0.0)),
        *_split_np(np.where(same_line, np.sin(last), 0.0)),
    )


def _mm3(a_hi, a_lo, b_hi, b_lo, dims=None):
    if dims is None:
        f = _dot
    else:
        f = lambda a, b: lax.dot_general(a, b, dims, preferred_element_type=F32)
    return f(a_hi, b_hi) + (f(a_hi, b_lo) + f(a_lo, b_hi))


NT = (((1,), (1,)), ((), ()))
LANE = 128


def dft_kernel(x_ref, c1h, c1l, s1h, s1l, twc_ref, tws_ref, bch, bcl, bsh, bsl, cos_ref, sin_ref):
    xh, xl = _split2(x_ref[...])
    y_re = _mm3(c1h[...], c1l[...], xh, xl)
    y_im = -_mm3(s1h[...], s1l[...], xh, xl)
    twc = twc_ref[...]
    tws = tws_ref[...]
    bc_h, bc_l, bs_h, bs_l = bch[...], bcl[...], bsh[...], bsl[...]
    norm_scale = 1.0 / math.sqrt(NX)
    blocks = x_ref.shape[0]
    lines_per_block = LANE // SUB
    for part in range(x_ref.shape[1] // LANE):
        cols = slice(part * LANE, (part + 1) * LANE)
        yr = y_re[:, cols]
        yi = y_im[:, cols]
        zrh, zrl = _split2(yr * twc + yi * tws)
        zih, zil = _split2(yi * twc - yr * tws)
        x_re = _mm3(bc_h, bc_l, zrh, zrl, NT) + _mm3(bs_h, bs_l, zih, zil, NT)
        x_neg_im = _mm3(bs_h, bs_l, zrh, zrl, NT) - _mm3(bc_h, bc_l, zih, zil, NT)
        rows = slice(part * lines_per_block, (part + 1) * lines_per_block)
        for f2 in range(cos_ref.shape[1] // blocks):
            picked = slice(f2 * lines_per_block, (f2 + 1) * lines_per_block)
            cos_ref[rows, f2 * blocks:(f2 + 1) * blocks] = x_re[picked] * norm_scale
            sin_ref[rows, f2 * blocks:(f2 + 1) * blocks] = x_neg_im[picked] * norm_scale


def line_spectra(x):
    blocks, width = x.shape
    lines = width // SUB
    f2_total = HALF // blocks
    tables = dft_tables(blocks, LANE // SUB, f2_total)
    out = jax.ShapeDtypeStruct((lines, HALF), F32)
    return pl.pallas_call(
        dft_kernel,
        out_shape=(out, out),
        cost_estimate=pl.CostEstimate(
            flops=2 * 3 * (2 * blocks * blocks * width + 4 * f2_total * width * blocks * LANE // SUB),
            bytes_accessed=4 * (blocks * width + 2 * lines * HALF + 2 * blocks * LANE) + 2 * 4 * blocks * blocks,
            transcendentals=0,
        ),
    )(x, *tables)


def body(velocity, new_owner, box_block, box_count, box_level):
    owners = lax.axis_size("own")
    groups = lax.axis_size("bulk")
    slot_total = velocity.shape[3]
    per_pair = slot_total // owners
    parcel_rows = owners * per_pair
    held_blocks = slot_total // 2
    first_block = lax.axis_index("bulk") * held_blocks
    slot_ids = jnp.arange(slot_total, dtype=jnp.int32)
    destination = new_owner[0, 0]
    filled = slot_ids < box_count[0, 0]
    same_owner = filled[:, None] & filled[None, :] & (destination[:, None] == destination[None, :])
    order_rank = jnp.sum((same_owner & (slot_ids[None, :] < slot_ids[:, None])).astype(jnp.int32), axis=1)
    row_of = jnp.where(filled, order_rank * owners + destination, parcel_rows)
    parcel_ids = jnp.arange(parcel_rows, dtype=jnp.int32)
    match = row_of[None, :] == parcel_ids[:, None]
    factor = level_factor(box_level[0, 0])
    source_safe = jnp.sum(jnp.where(match, slot_ids[None, :], 0), axis=1)
    row_factor = jnp.sum(jnp.where(match, factor[None, :], 0.0), axis=1)
    row_block = jnp.sum(jnp.where(match, box_block[0, 0][None, :] + 1, 0), axis=1) - 1
    code_lanes = jnp.arange(CODE_W, dtype=jnp.int32)
    by_owner = row_block.reshape(per_pair, owners).T
    codes = jnp.where(
        code_lanes[None, :] < per_pair,
        jnp.take(by_owner, jnp.minimum(code_lanes, per_pair - 1), axis=1),
        -1,
    ).astype(F32)

    parcel = source_divergence(velocity[:, 0, 0], source_safe, row_factor, codes, groups)

    arrived = lax.all_to_all(parcel, ("bulk", "own"), split_axis=0, concat_axis=0, tiled=True)
    piece_w = BOX * FACE // groups
    data_w = piece_w * per_pair
    code_in = arrived[:, data_w:data_w + per_pair].reshape(-1)
    total_blocks = groups * held_blocks
    place_at = jnp.where(code_in >= 0, code_in.astype(jnp.int32), total_blocks)
    arrived_ids = jnp.arange(code_in.shape[0], dtype=jnp.int32)
    block_ids = jnp.arange(total_blocks, dtype=jnp.int32)
    chosen = jnp.sum(jnp.where(place_at[None, :] == block_ids[:, None], arrived_ids[None, :], 0), axis=1)
    pieces = arrived[:, :data_w].reshape(-1, piece_w)
    cosine, sine_vals = line_spectra(jnp.take(pieces, chosen, axis=0))
    return (cosine[None], sine_vals[None])


def solution(mesh):
    in_specs = (
        P(None, "bulk", "own", None, None),
        P("bulk", "own", None),
        P("bulk", "own", None),
        P("bulk", "own"),
        P("bulk", "own", None),
    )
    out_specs = (P("own", "bulk", None), P("own", "bulk", None))
    return jax.shard_map(body, mesh=mesh, in_specs=in_specs, out_specs=out_specs, check_vma=False)
```

```python
import math

import ml_dtypes
import numpy as np

import jax
import jax.numpy as jnp
from jax import lax
from jax.experimental import pallas as pl
from jax.experimental.pallas import tpu as pltpu
from jax.sharding import PartitionSpec as P

BOX = 16
GHOST = BOX + 2
PLANE = GHOST * GHOST
PLANE_PAD = 384
FACE = BOX * BOX
HALF = 3072
NX = 6144
SUB = 16
CODE_W = 128

HIGHEST = lax.Precision.HIGHEST
F32 = jnp.float32
BF16 = jnp.bfloat16


def level_factor(level):
    return jnp.where(level == 1, 0.5, jnp.where(level == 2, 1.0, 2.0)).astype(jnp.float32)


def selection_table():
    sel = np.zeros((PLANE_PAD, FACE), np.float32)
    for j in range(BOX):
        for k in range(BOX):
            sel[GHOST * (j + 1) + k + 1, j * BOX + k] = 1.0
    return jnp.asarray(sel, BF16)


def _split2(x):
    hi = x.astype(BF16)
    lo = (x - hi.astype(F32)).astype(BF16)
    return hi, lo


def _split3(x):
    hi = x.astype(BF16)
    rest = x - hi.astype(F32)
    mid = rest.astype(BF16)
    lo = (rest - mid.astype(F32)).astype(BF16)
    return hi, mid, lo


def _dot(a, b):
    return jnp.dot(a, b, preferred_element_type=F32)


def _exact_right(x, m):
    hi, mid, lo = _split3(x)
    return _dot(hi, m) + _dot(mid, m) + _dot(lo, m)


def _exact_left(m, x):
    hi, mid, lo = _split3(x)
    return _dot(m, hi) + _dot(m, mid) + _dot(m, lo)


WINDOW = 512
ROW_PAD = 6016


def _plane(x_ref, field, p):
    start = PLANE * p
    base = (start // 128) * 128
    off = start - base
    w = x_ref[field, :, base:base + WINDOW]
    if off:
        w = pltpu.roll(w, WINDOW - off, 1)
    return w[:, :PLANE_PAD]


TAIL_BASE = 5376


def divergence_kernel(src_ref, x_hbm, tail_hbm, sel_ref, fac_ref, code_ref, o_ref, buf, buf_tail, sem):
    owners = code_ref.shape[0]
    per_pair = src_ref.shape[0] // owners
    chunk_rows = o_ref.shape[0]
    data_w = o_ref.shape[1] - code_ref.shape[1]
    groups = chunk_rows // owners
    planes_per_group = BOX // groups
    piece_w = data_w // per_pair

    def fetch(t, slot):
        for r in range(owners):
            row = src_ref[t * owners + r]
            pltpu.make_async_copy(
                x_hbm.at[:, pl.ds(row, 1), :], buf.at[slot, :, pl.ds(r, 1), :], sem.at[slot, 0]
            ).start()
            pltpu.make_async_copy(
                tail_hbm.at[pl.ds(row, 1), :], buf_tail.at[slot, pl.ds(r, 1), :], sem.at[slot, 1]
            ).start()

    def wait(slot):
        pltpu.make_async_copy(x_hbm.at[:, pl.ds(0, owners), :], buf.at[slot], sem.at[slot, 0]).wait()
        pltpu.make_async_copy(tail_hbm.at[pl.ds(0, owners), :], buf_tail.at[slot], sem.at[slot, 1]).wait()

    fetch(0, 0)
    for g in range(groups):
        o_ref[g * owners:(g + 1) * owners, data_w:] = code_ref[...]
    sel = sel_ref[...]
    last = GHOST - 1
    for t in range(per_pair):
        slot = t % 2
        if t + 1 < per_pair:
            fetch(t + 1, 1 - slot)
        wait(slot)
        x_ref = buf.at[slot]
        v_planes = [_plane(x_ref, 1, p) for p in range(last)]
        tail = pltpu.roll(buf_tail[slot], WINDOW - (PLANE * last - TAIL_BASE), 1)
        v_planes.append(tail[:, :PLANE_PAD])
        pieces = []
        for i in range(BOX):
            u = _plane(x_ref, 0, i + 1)
            w = _plane(x_ref, 2, i + 1)
            along_x = pltpu.roll(u, PLANE_PAD - 1, 1) - pltpu.roll(u, 1, 1)
            along_y = v_planes[i + 2] - v_planes[i]
            along_z = pltpu.roll(w, PLANE_PAD - GHOST, 1) - pltpu.roll(w, GHOST, 1)
            pieces.append(along_x + (along_y + along_z))
        interior = _exact_right(jnp.concatenate(pieces, axis=0), sel)
        fac = fac_ref[t * owners:(t + 1) * owners, :]
        for i in range(BOX):
            g, half = divmod(i, planes_per_group)
            lane0 = t * piece_w + half * FACE
            o_ref[g * owners:(g + 1) * owners, lane0:lane0 + FACE] = interior[i * owners:(i + 1) * owners] * fac


def source_divergence(cells, source, factor, codes, groups):
    slots = cells.shape[1]
    owners = codes.shape[0]
    out_w = BOX * FACE // groups * (slots // owners) + CODE_W
    sel = selection_table()
    tail = jnp.pad(cells[1, :, TAIL_BASE:], ((0, 0), (0, TAIL_BASE + WINDOW - cells.shape[-1])))
    vmem = pl.BlockSpec(memory_space=pltpu.VMEM)
    return pl.pallas_call(
        divergence_kernel,
        in_specs=[
            pl.BlockSpec(memory_space=pltpu.SMEM),
            pl.BlockSpec(memory_space=pl.ANY),
            pl.BlockSpec(memory_space=pl.ANY),
            vmem,
            vmem,
            vmem,
        ],
        out_specs=vmem,
        out_shape=jax.ShapeDtypeStruct((groups * owners, out_w), F32),
        scratch_shapes=[
            pltpu.VMEM((2, 3, owners, cells.shape[2]), F32),
            pltpu.VMEM((2, owners, WINDOW), F32),
            pltpu.SemaphoreType.DMA((2, 2)),
        ],
        cost_estimate=pl.CostEstimate(
            flops=2 * slots * BOX * PLANE_PAD * FACE * 3,
            bytes_accessed=4 * (3 * slots * ROW_PAD + groups * owners * out_w),
            transcendentals=0,
        ),
    )(source, cells, tail, sel, jnp.broadcast_to(factor[:, None], (slots, FACE)), codes)


def _split_np(t):
    hi = t.astype(ml_dtypes.bfloat16)
    lo = (t - hi.astype(np.float64)).astype(ml_dtypes.bfloat16)
    return jnp.asarray(hi), jnp.asarray(lo)


def _angles(product, period):
    return (2.0 * np.pi / period) * (product % period).astype(np.float64)


def dft_tables(blocks, lines_per_block, f2_total):
    g_ids = np.arange(blocks, dtype=np.int64)
    stage_one = _angles(g_ids[:, None] * g_ids[None, :], blocks)
    lanes = lines_per_block * SUB
    twist = _angles(g_ids[:, None] * (np.arange(lanes) % SUB)[None, :], NX)
    row = np.arange(f2_total * lines_per_block)
    col = np.arange(lanes)
    same_line = (row[:, None] % lines_per_block) == (col[None, :] // SUB)
    last = _angles((row[:, None] // lines_per_block) * (col[None, :] % SUB), SUB)
    return (
        *_split_np(np.cos(stage_one)),
        *_split_np(np.sin(stage_one)),
        jnp.asarray(np.cos(twist), F32),
        jnp.asarray(np.sin(twist), F32),
        *_split_np(np.where(same_line, np.cos(last), 0.0)),
        *_split_np(np.where(same_line, np.sin(last), 0.0)),
    )


def _mm3(a_hi, a_lo, b_hi, b_lo, dims=None):
    if dims is None:
        f = _dot
    else:
        f = lambda a, b: lax.dot_general(a, b, dims, preferred_element_type=F32)
    return f(a_hi, b_hi) + (f(a_hi, b_lo) + f(a_lo, b_hi))


NT = (((1,), (1,)), ((), ()))
LANE = 128


def dft_kernel(x_ref, c1h, c1l, s1h, s1l, twc_ref, tws_ref, bch, bcl, bsh, bsl, cos_ref, sin_ref):
    xh, xl = _split2(x_ref[...])
    y_re = _mm3(c1h[...], c1l[...], xh, xl)
    y_im = -_mm3(s1h[...], s1l[...], xh, xl)
    twc = twc_ref[...]
    tws = tws_ref[...]
    bc_h, bc_l, bs_h, bs_l = bch[...], bcl[...], bsh[...], bsl[...]
    norm_scale = 1.0 / math.sqrt(NX)
    blocks = x_ref.shape[0]
    lines_per_block = LANE // SUB
    for part in range(x_ref.shape[1] // LANE):
        cols = slice(part * LANE, (part + 1) * LANE)
        yr = y_re[:, cols]
        yi = y_im[:, cols]
        zrh, zrl = _split2(yr * twc + yi * tws)
        zih, zil = _split2(yi * twc - yr * tws)
        x_re = _mm3(bc_h, bc_l, zrh, zrl, NT) + _mm3(bs_h, bs_l, zih, zil, NT)
        x_neg_im = _mm3(bs_h, bs_l, zrh, zrl, NT) - _mm3(bc_h, bc_l, zih, zil, NT)
        rows = slice(part * lines_per_block, (part + 1) * lines_per_block)
        for f2 in range(cos_ref.shape[1] // blocks):
            picked = slice(f2 * lines_per_block, (f2 + 1) * lines_per_block)
            cos_ref[rows, f2 * blocks:(f2 + 1) * blocks] = x_re[picked] * norm_scale
            sin_ref[rows, f2 * blocks:(f2 + 1) * blocks] = x_neg_im[picked] * norm_scale


def line_spectra(x):
    blocks, width = x.shape
    lines = width // SUB
    f2_total = HALF // blocks
    tables = dft_tables(blocks, LANE // SUB, f2_total)
    out = jax.ShapeDtypeStruct((lines, HALF), F32)
    return pl.pallas_call(
        dft_kernel,
        out_shape=(out, out),
        cost_estimate=pl.CostEstimate(
            flops=2 * 3 * (2 * blocks * blocks * width + 4 * f2_total * width * blocks * LANE // SUB),
            bytes_accessed=4 * (blocks * width + 2 * lines * HALF + 2 * blocks * LANE) + 2 * 4 * blocks * blocks,
            transcendentals=0,
        ),
    )(x, *tables)


def body(velocity, new_owner, box_block, box_count, box_level):
    owners = lax.axis_size("own")
    groups = lax.axis_size("bulk")
    slot_total = velocity.shape[3]
    per_pair = slot_total // owners
    parcel_rows = owners * per_pair
    held_blocks = slot_total // 2
    first_block = lax.axis_index("bulk") * held_blocks
    slot_ids = jnp.arange(slot_total, dtype=jnp.int32)
    destination = new_owner[0, 0]
    filled = slot_ids < box_count[0, 0]
    same_owner = filled[:, None] & filled[None, :] & (destination[:, None] == destination[None, :])
    order_rank = jnp.sum((same_owner & (slot_ids[None, :] < slot_ids[:, None])).astype(jnp.int32), axis=1)
    row_of = jnp.where(filled, order_rank * owners + destination, parcel_rows)
    parcel_ids = jnp.arange(parcel_rows, dtype=jnp.int32)
    match = row_of[None, :] == parcel_ids[:, None]
    factor = level_factor(box_level[0, 0])
    source_safe = jnp.sum(jnp.where(match, slot_ids[None, :], 0), axis=1)
    row_factor = jnp.sum(jnp.where(match, factor[None, :], 0.0), axis=1)
    row_block = jnp.sum(jnp.where(match, box_block[0, 0][None, :] + 1, 0), axis=1) - 1
    code_lanes = jnp.arange(CODE_W, dtype=jnp.int32)
    by_owner = row_block.reshape(per_pair, owners).T
    codes = jnp.where(
        code_lanes[None, :] < per_pair,
        jnp.take(by_owner, jnp.minimum(code_lanes, per_pair - 1), axis=1),
        -1,
    ).astype(F32)

    parcel = source_divergence(velocity[:, 0, 0], source_safe, row_factor, codes, groups)

    arrived = lax.all_to_all(parcel, ("bulk", "own"), split_axis=0, concat_axis=0, tiled=True)
    piece_w = BOX * FACE // groups
    data_w = piece_w * per_pair
    code_in = arrived[:, data_w:data_w + per_pair].reshape(-1)
    total_blocks = groups * held_blocks
    place_at = jnp.where(code_in >= 0, code_in.astype(jnp.int32), total_blocks)
    arrived_ids = jnp.arange(code_in.shape[0], dtype=jnp.int32)
    block_ids = jnp.arange(total_blocks, dtype=jnp.int32)
    chosen = jnp.sum(jnp.where(place_at[None, :] == block_ids[:, None], arrived_ids[None, :], 0), axis=1)
    pieces = arrived[:, :data_w].reshape(-1, piece_w)
    cosine, sine_vals = line_spectra(jnp.take(pieces, chosen, axis=0))
    return (cosine[None], sine_vals[None])


def solution(mesh):
    in_specs = (
        P(None, "bulk", "own", None, None),
        P("bulk", "own", None),
        P("bulk", "own", None),
        P("bulk", "own"),
        P("bulk", "own", None),
    )
    out_specs = (P("own", "bulk", None), P("own", "bulk", None))
    return jax.shard_map(body, mesh=mesh, in_specs=in_specs, out_specs=out_specs, check_vma=False)
```

```python
import math

import ml_dtypes
import numpy as np

import jax
import jax.numpy as jnp
from jax import lax
from jax.experimental import pallas as pl
from jax.experimental.pallas import tpu as pltpu
from jax.sharding import PartitionSpec as P

BOX = 16
GHOST = BOX + 2
PLANE = GHOST * GHOST
PLANE_PAD = 384
FACE = BOX * BOX
HALF = 3072
NX = 6144
SUB = 16
CODE_W = 128

HIGHEST = lax.Precision.HIGHEST
F32 = jnp.float32
BF16 = jnp.bfloat16


def level_factor(level):
    return jnp.where(level == 1, 0.5, jnp.where(level == 2, 1.0, 2.0)).astype(jnp.float32)


def selection_table():
    sel = np.zeros((PLANE_PAD, FACE), np.float32)
    for j in range(BOX):
        for k in range(BOX):
            sel[GHOST * (j + 1) + k + 1, j * BOX + k] = 1.0
    return jnp.asarray(sel, BF16)


def _split2(x):
    hi = x.astype(BF16)
    lo = (x - hi.astype(F32)).astype(BF16)
    return hi, lo


def _split3(x):
    hi = x.astype(BF16)
    rest = x - hi.astype(F32)
    mid = rest.astype(BF16)
    lo = (rest - mid.astype(F32)).astype(BF16)
    return hi, mid, lo


def _dot(a, b):
    return jnp.dot(a, b, preferred_element_type=F32)


def _exact_right(x, m):
    hi, mid, lo = _split3(x)
    return _dot(hi, m) + _dot(mid, m) + _dot(lo, m)


def _exact_left(m, x):
    hi, mid, lo = _split3(x)
    return _dot(m, hi) + _dot(m, mid) + _dot(m, lo)


WINDOW = 512
ROW_PAD = 6016


def _plane(x_ref, field, p):
    start = PLANE * p
    base = (start // 128) * 128
    off = start - base
    w = x_ref[field, :, base:base + WINDOW]
    if off:
        w = pltpu.roll(w, WINDOW - off, 1)
    return w[:, :PLANE_PAD]


TAIL_BASE = 5376


def divergence_kernel(src_ref, x_hbm, tail_hbm, sel_ref, fac_ref, code_ref, o_ref, buf, buf_tail, sem):
    owners = code_ref.shape[0]
    per_pair = src_ref.shape[0] // owners
    chunk_rows = o_ref.shape[0]
    data_w = o_ref.shape[1] - code_ref.shape[1]
    groups = chunk_rows // owners
    planes_per_group = BOX // groups
    piece_w = data_w // per_pair

    def fetch(t, slot):
        for r in range(owners):
            row = src_ref[t * owners + r]
            pltpu.make_async_copy(
                x_hbm.at[:, pl.ds(row, 1), :], buf.at[slot, :, pl.ds(r, 1), :], sem.at[slot, 0]
            ).start()
            pltpu.make_async_copy(
                tail_hbm.at[pl.ds(row, 1), :], buf_tail.at[slot, pl.ds(r, 1), :], sem.at[slot, 1]
            ).start()

    def wait(slot):
        pltpu.make_async_copy(x_hbm.at[:, pl.ds(0, owners), :], buf.at[slot], sem.at[slot, 0]).wait()
        pltpu.make_async_copy(tail_hbm.at[pl.ds(0, owners), :], buf_tail.at[slot], sem.at[slot, 1]).wait()

    fetch(0, 0)
    for g in range(groups):
        o_ref[g * owners:(g + 1) * owners, data_w:] = code_ref[...]
    sel = sel_ref[...]
    last = GHOST - 1
    for t in range(per_pair):
        slot = t % 2
        if t + 1 < per_pair:
            fetch(t + 1, 1 - slot)
        wait(slot)
        x_ref = buf.at[slot]
        v_planes = [_plane(x_ref, 1, p) for p in range(last)]
        tail = pltpu.roll(buf_tail[slot], WINDOW - (PLANE * last - TAIL_BASE), 1)
        v_planes.append(tail[:, :PLANE_PAD])
        pieces = []
        for i in range(BOX):
            u = _plane(x_ref, 0, i + 1)
            w = _plane(x_ref, 2, i + 1)
            along_x = pltpu.roll(u, PLANE_PAD - 1, 1) - pltpu.roll(u, 1, 1)
            along_y = v_planes[i + 2] - v_planes[i]
            along_z = pltpu.roll(w, PLANE_PAD - GHOST, 1) - pltpu.roll(w, GHOST, 1)
            pieces.append(along_x + (along_y + along_z))
        interior = _exact_right(jnp.concatenate(pieces, axis=0), sel)
        fac = fac_ref[t * owners:(t + 1) * owners, :]
        for i in range(BOX):
            g, half = divmod(i, planes_per_group)
            lane0 = t * piece_w + half * FACE
            o_ref[g * owners:(g + 1) * owners, lane0:lane0 + FACE] = interior[i * owners:(i + 1) * owners] * fac


def source_divergence(cells, source, factor, codes, groups):
    slots = cells.shape[1]
    owners = codes.shape[0]
    out_w = BOX * FACE // groups * (slots // owners) + CODE_W
    sel = selection_table()
    tail = jnp.pad(cells[1, :, TAIL_BASE:], ((0, 0), (0, TAIL_BASE + WINDOW - cells.shape[-1])))
    vmem = pl.BlockSpec(memory_space=pltpu.VMEM)
    return pl.pallas_call(
        divergence_kernel,
        in_specs=[
            pl.BlockSpec(memory_space=pltpu.SMEM),
            pl.BlockSpec(memory_space=pl.ANY),
            pl.BlockSpec(memory_space=pl.ANY),
            vmem,
            vmem,
            vmem,
        ],
        out_specs=vmem,
        out_shape=jax.ShapeDtypeStruct((groups * owners, out_w), F32),
        scratch_shapes=[
            pltpu.VMEM((2, 3, owners, cells.shape[2]), F32),
            pltpu.VMEM((2, owners, WINDOW), F32),
            pltpu.SemaphoreType.DMA((2, 2)),
        ],
        cost_estimate=pl.CostEstimate(
            flops=2 * slots * BOX * PLANE_PAD * FACE * 3,
            bytes_accessed=4 * (3 * slots * ROW_PAD + groups * owners * out_w),
            transcendentals=0,
        ),
    )(source, cells, tail, sel, jnp.broadcast_to(factor[:, None], (slots, FACE)), codes)


def _split_np(t):
    hi = t.astype(ml_dtypes.bfloat16)
    lo = (t - hi.astype(np.float64)).astype(ml_dtypes.bfloat16)
    return jnp.asarray(hi), jnp.asarray(lo)


def _angles(product, period):
    return (2.0 * np.pi / period) * (product % period).astype(np.float64)


def dft_tables(blocks, lines_per_block, f2_total):
    g_ids = np.arange(blocks, dtype=np.int64)
    stage_one = _angles(g_ids[:, None] * g_ids[None, :], blocks)
    lanes = lines_per_block * SUB
    twist = _angles(g_ids[:, None] * (np.arange(lanes) % SUB)[None, :], NX)
    row = np.arange(f2_total * lines_per_block)
    col = np.arange(lanes)
    same_line = (row[:, None] % lines_per_block) == (col[None, :] // SUB)
    last = _angles((row[:, None] // lines_per_block) * (col[None, :] % SUB), SUB)
    return (
        *_split_np(np.cos(stage_one)),
        *_split_np(np.sin(stage_one)),
        jnp.asarray(np.cos(twist), F32),
        jnp.asarray(np.sin(twist), F32),
        *_split_np(np.where(same_line, np.cos(last), 0.0)),
        *_split_np(np.where(same_line, np.sin(last), 0.0)),
    )


def _mm3(a_hi, a_lo, b_hi, b_lo, dims=None):
    if dims is None:
        f = _dot
    else:
        f = lambda a, b: lax.dot_general(a, b, dims, preferred_element_type=F32)
    return f(a_hi, b_hi) + (f(a_hi, b_lo) + f(a_lo, b_hi))


NT = (((1,), (1,)), ((), ()))
LANE = 128


def dft_kernel(x_ref, c1h, c1l, s1h, s1l, twc_ref, tws_ref, bch, bcl, bsh, bsl, cos_ref, sin_ref):
    xh, xl = _split2(x_ref[...])
    y_re = _mm3(c1h[...], c1l[...], xh, xl)
    y_im = -_mm3(s1h[...], s1l[...], xh, xl)
    twc = twc_ref[...]
    tws = tws_ref[...]
    bc_h, bc_l, bs_h, bs_l = bch[...], bcl[...], bsh[...], bsl[...]
    norm_scale = 1.0 / math.sqrt(NX)
    blocks = x_ref.shape[0]
    lines_per_block = LANE // SUB
    for part in range(x_ref.shape[1] // LANE):
        cols = slice(part * LANE, (part + 1) * LANE)
        yr = y_re[:, cols]
        yi = y_im[:, cols]
        zrh, zrl = _split2(yr * twc + yi * tws)
        zih, zil = _split2(yi * twc - yr * tws)
        x_re = _mm3(bc_h, bc_l, zrh, zrl, NT) + _mm3(bs_h, bs_l, zih, zil, NT)
        x_neg_im = _mm3(bs_h, bs_l, zrh, zrl, NT) - _mm3(bc_h, bc_l, zih, zil, NT)
        rows = slice(part * lines_per_block, (part + 1) * lines_per_block)
        for f2 in range(cos_ref.shape[1] // blocks):
            picked = slice(f2 * lines_per_block, (f2 + 1) * lines_per_block)
            cos_ref[rows, f2 * blocks:(f2 + 1) * blocks] = x_re[picked] * norm_scale
            sin_ref[rows, f2 * blocks:(f2 + 1) * blocks] = x_neg_im[picked] * norm_scale


def line_spectra(x):
    blocks, width = x.shape
    lines = width // SUB
    f2_total = HALF // blocks
    tables = dft_tables(blocks, LANE // SUB, f2_total)
    out = jax.ShapeDtypeStruct((lines, HALF), F32)
    return pl.pallas_call(
        dft_kernel,
        out_shape=(out, out),
        cost_estimate=pl.CostEstimate(
            flops=2 * 3 * (2 * blocks * blocks * width + 4 * f2_total * width * blocks * LANE // SUB),
            bytes_accessed=4 * (blocks * width + 2 * lines * HALF + 2 * blocks * LANE) + 2 * 4 * blocks * blocks,
            transcendentals=0,
        ),
    )(x, *tables)


def body(velocity, new_owner, box_block, box_count, box_level):
    owners = lax.axis_size("own")
    groups = lax.axis_size("bulk")
    slot_total = velocity.shape[3]
    per_pair = slot_total // owners
    parcel_rows = owners * per_pair
    held_blocks = slot_total // 2
    first_block = lax.axis_index("bulk") * held_blocks
    slot_ids = jnp.arange(slot_total, dtype=jnp.int32)
    destination = new_owner[0, 0]
    filled = slot_ids < box_count[0, 0]
    same_owner = filled[:, None] & filled[None, :] & (destination[:, None] == destination[None, :])
    order_rank = jnp.sum((same_owner & (slot_ids[None, :] < slot_ids[:, None])).astype(jnp.int32), axis=1)
    row_of = jnp.where(filled, order_rank * owners + destination, parcel_rows)
    parcel_ids = jnp.arange(parcel_rows, dtype=jnp.int32)
    match = row_of[None, :] == parcel_ids[:, None]
    factor = level_factor(box_level[0, 0])
    source_safe = jnp.sum(jnp.where(match, slot_ids[None, :], 0), axis=1)
    row_factor = jnp.sum(jnp.where(match, factor[None, :], 0.0), axis=1)
    row_block = jnp.sum(jnp.where(match, box_block[0, 0][None, :] + 1, 0), axis=1) - 1
    code_lanes = jnp.arange(CODE_W, dtype=jnp.int32)
    by_owner = row_block.reshape(per_pair, owners).T
    codes = jnp.where(
        code_lanes[None, :] < per_pair,
        jnp.take(by_owner, jnp.minimum(code_lanes, per_pair - 1), axis=1),
        -1,
    ).astype(F32)

    parcel = source_divergence(velocity[:, 0, 0], source_safe, row_factor, codes, groups)

    arrived = lax.all_to_all(parcel, ("bulk", "own"), split_axis=0, concat_axis=0, tiled=True)
    piece_w = BOX * FACE // groups
    data_w = piece_w * per_pair
    code_in = arrived[:, data_w:data_w + per_pair].reshape(-1)
    total_blocks = groups * held_blocks
    place_at = jnp.where(code_in >= 0, code_in.astype(jnp.int32), total_blocks)
    arrived_ids = jnp.arange(code_in.shape[0], dtype=jnp.int32)
    block_ids = jnp.arange(total_blocks, dtype=jnp.int32)
    chosen = jnp.sum(jnp.where(place_at[None, :] == block_ids[:, None], arrived_ids[None, :], 0), axis=1)
    pieces = arrived[:, :data_w].reshape(-1, piece_w)
    cosine, sine_vals = line_spectra(jnp.take(pieces, chosen, axis=0, mode="clip"))
    return (cosine[None], sine_vals[None])


def solution(mesh):
    in_specs = (
        P(None, "bulk", "own", None, None),
        P("bulk", "own", None),
        P("bulk", "own", None),
        P("bulk", "own"),
        P("bulk", "own", None),
    )
    out_specs = (P("own", "bulk", None), P("own", "bulk", None))
    return jax.shard_map(body, mesh=mesh, in_specs=in_specs, out_specs=out_specs, check_vma=False)
```

```python
import math

import ml_dtypes
import numpy as np

import jax
import jax.numpy as jnp
from jax import lax
from jax.experimental import pallas as pl
from jax.experimental.pallas import tpu as pltpu
from jax.sharding import PartitionSpec as P

BOX = 16
GHOST = BOX + 2
PLANE = GHOST * GHOST
PLANE_PAD = 384
FACE = BOX * BOX
HALF = 3072
NX = 6144
SUB = 16
CODE_W = 128

HIGHEST = lax.Precision.HIGHEST
F32 = jnp.float32
BF16 = jnp.bfloat16


def level_factor(level):
    return jnp.where(level == 1, 0.5, jnp.where(level == 2, 1.0, 2.0)).astype(jnp.float32)


def selection_table():
    sel = np.zeros((PLANE_PAD, FACE), np.float32)
    for j in range(BOX):
        for k in range(BOX):
            sel[GHOST * (j + 1) + k + 1, j * BOX + k] = 1.0
    return jnp.asarray(sel, BF16)


def _split2(x):
    hi = x.astype(BF16)
    lo = (x - hi.astype(F32)).astype(BF16)
    return hi, lo


def _split3(x):
    hi = x.astype(BF16)
    rest = x - hi.astype(F32)
    mid = rest.astype(BF16)
    lo = (rest - mid.astype(F32)).astype(BF16)
    return hi, mid, lo


def _dot(a, b):
    return jnp.dot(a, b, preferred_element_type=F32)


def _exact_right(x, m):
    hi, mid, lo = _split3(x)
    return _dot(hi, m) + _dot(mid, m) + _dot(lo, m)


def _exact_left(m, x):
    hi, mid, lo = _split3(x)
    return _dot(m, hi) + _dot(m, mid) + _dot(m, lo)


WINDOW = 512
ROW_PAD = 6016


def _plane(x_ref, field, p):
    start = PLANE * p
    base = (start // 128) * 128
    off = start - base
    w = x_ref[field, :, base:base + WINDOW]
    if off:
        w = pltpu.roll(w, WINDOW - off, 1)
    return w[:, :PLANE_PAD]


TAIL_BASE = 5376


def divergence_kernel(src_ref, x_hbm, tail_hbm, sel_ref, fac_ref, code_ref, o_ref, buf, buf_tail, sem):
    owners = code_ref.shape[0]
    per_pair = src_ref.shape[0] // owners
    chunk_rows = o_ref.shape[0]
    data_w = o_ref.shape[1] - code_ref.shape[1]
    groups = chunk_rows // owners
    planes_per_group = BOX // groups
    piece_w = data_w // per_pair

    def fetch(t, slot):
        for r in range(owners):
            row = src_ref[t * owners + r]
            pltpu.make_async_copy(
                x_hbm.at[:, pl.ds(row, 1), :], buf.at[slot, :, pl.ds(r, 1), :], sem.at[slot, 0]
            ).start()
            pltpu.make_async_copy(
                tail_hbm.at[pl.ds(row, 1), :], buf_tail.at[slot, pl.ds(r, 1), :], sem.at[slot, 1]
            ).start()

    def wait(slot):
        pltpu.make_async_copy(x_hbm.at[:, pl.ds(0, owners), :], buf.at[slot], sem.at[slot, 0]).wait()
        pltpu.make_async_copy(tail_hbm.at[pl.ds(0, owners), :], buf_tail.at[slot], sem.at[slot, 1]).wait()

    fetch(0, 0)
    for g in range(groups):
        o_ref[g * owners:(g + 1) * owners, data_w:] = code_ref[...]
    sel = sel_ref[...]
    last = GHOST - 1
    for t in range(per_pair):
        slot = t % 2
        if t + 1 < per_pair:
            fetch(t + 1, 1 - slot)
        wait(slot)
        x_ref = buf.at[slot]
        v_planes = [_plane(x_ref, 1, p) for p in range(last)]
        tail = pltpu.roll(buf_tail[slot], WINDOW - (PLANE * last - TAIL_BASE), 1)
        v_planes.append(tail[:, :PLANE_PAD])
        pieces = []
        for i in range(BOX):
            u = _plane(x_ref, 0, i + 1)
            w = _plane(x_ref, 2, i + 1)
            along_x = pltpu.roll(u, PLANE_PAD - 1, 1) - pltpu.roll(u, 1, 1)
            along_y = v_planes[i + 2] - v_planes[i]
            along_z = pltpu.roll(w, PLANE_PAD - GHOST, 1) - pltpu.roll(w, GHOST, 1)
            pieces.append(along_x + (along_y + along_z))
        hi, lo = _split2(jnp.concatenate(pieces, axis=0))
        interior = _dot(hi, sel) + _dot(lo, sel)
        fac = fac_ref[t * owners:(t + 1) * owners, :]
        for i in range(BOX):
            g, half = divmod(i, planes_per_group)
            lane0 = t * piece_w + half * FACE
            o_ref[g * owners:(g + 1) * owners, lane0:lane0 + FACE] = interior[i * owners:(i + 1) * owners] * fac


def source_divergence(cells, source, factor, codes, groups):
    slots = cells.shape[1]
    owners = codes.shape[0]
    out_w = BOX * FACE // groups * (slots // owners) + CODE_W
    sel = selection_table()
    tail = jnp.pad(cells[1, :, TAIL_BASE:], ((0, 0), (0, TAIL_BASE + WINDOW - cells.shape[-1])))
    vmem = pl.BlockSpec(memory_space=pltpu.VMEM)
    return pl.pallas_call(
        divergence_kernel,
        in_specs=[
            pl.BlockSpec(memory_space=pltpu.SMEM),
            pl.BlockSpec(memory_space=pl.ANY),
            pl.BlockSpec(memory_space=pl.ANY),
            vmem,
            vmem,
            vmem,
        ],
        out_specs=vmem,
        out_shape=jax.ShapeDtypeStruct((groups * owners, out_w), F32),
        scratch_shapes=[
            pltpu.VMEM((2, 3, owners, cells.shape[2]), F32),
            pltpu.VMEM((2, owners, WINDOW), F32),
            pltpu.SemaphoreType.DMA((2, 2)),
        ],
        cost_estimate=pl.CostEstimate(
            flops=2 * slots * BOX * PLANE_PAD * FACE * 3,
            bytes_accessed=4 * (3 * slots * ROW_PAD + groups * owners * out_w),
            transcendentals=0,
        ),
    )(source, cells, tail, sel, factor[:, None], codes)


def _split_np(t):
    hi = t.astype(ml_dtypes.bfloat16)
    lo = (t - hi.astype(np.float64)).astype(ml_dtypes.bfloat16)
    return jnp.asarray(hi), jnp.asarray(lo)


def _angles(product, period):
    return (2.0 * np.pi / period) * (product % period).astype(np.float64)


def dft_tables(blocks, lines_per_block, f2_total):
    g_ids = np.arange(blocks, dtype=np.int64)
    stage_one = _angles(g_ids[:, None] * g_ids[None, :], blocks)
    lanes = lines_per_block * SUB
    twist = _angles(g_ids[:, None] * (np.arange(lanes) % SUB)[None, :], NX)
    row = np.arange(f2_total * lines_per_block)
    col = np.arange(lanes)
    same_line = (row[:, None] % lines_per_block) == (col[None, :] // SUB)
    last = _angles((row[:, None] // lines_per_block) * (col[None, :] % SUB), SUB)
    return (
        *_split_np(np.cos(stage_one)),
        *_split_np(np.sin(stage_one)),
        jnp.asarray(np.cos(twist), F32),
        jnp.asarray(np.sin(twist), F32),
        *_split_np(np.where(same_line, np.cos(last), 0.0)),
        *_split_np(np.where(same_line, np.sin(last), 0.0)),
    )


def _mm3(a_hi, a_lo, b_hi, b_lo, dims=None):
    if dims is None:
        f = _dot
    else:
        f = lambda a, b: lax.dot_general(a, b, dims, preferred_element_type=F32)
    return f(a_hi, b_hi) + (f(a_hi, b_lo) + f(a_lo, b_hi))


NT = (((1,), (1,)), ((), ()))
LANE = 128


def dft_kernel(x_ref, c1h, c1l, s1h, s1l, twc_ref, tws_ref, bch, bcl, bsh, bsl, cos_ref, sin_ref):
    xh, xl = _split2(x_ref[...])
    y_re = _mm3(c1h[...], c1l[...], xh, xl)
    y_im = -_mm3(s1h[...], s1l[...], xh, xl)
    twc = twc_ref[...]
    tws = tws_ref[...]
    bc_h, bc_l, bs_h, bs_l = bch[...], bcl[...], bsh[...], bsl[...]
    norm_scale = 1.0 / math.sqrt(NX)
    blocks = x_ref.shape[0]
    lines_per_block = LANE // SUB
    for part in range(x_ref.shape[1] // LANE):
        cols = slice(part * LANE, (part + 1) * LANE)
        yr = y_re[:, cols]
        yi = y_im[:, cols]
        zrh, zrl = _split2(yr * twc + yi * tws)
        zih, zil = _split2(yi * twc - yr * tws)
        x_re = _mm3(bc_h, bc_l, zrh, zrl, NT) + _mm3(bs_h, bs_l, zih, zil, NT)
        x_neg_im = _mm3(bs_h, bs_l, zrh, zrl, NT) - _mm3(bc_h, bc_l, zih, zil, NT)
        rows = slice(part * lines_per_block, (part + 1) * lines_per_block)
        for f2 in range(cos_ref.shape[1] // blocks):
            picked = slice(f2 * lines_per_block, (f2 + 1) * lines_per_block)
            cos_ref[rows, f2 * blocks:(f2 + 1) * blocks] = x_re[picked] * norm_scale
            sin_ref[rows, f2 * blocks:(f2 + 1) * blocks] = x_neg_im[picked] * norm_scale


def line_spectra(x):
    blocks, width = x.shape
    lines = width // SUB
    f2_total = HALF // blocks
    tables = dft_tables(blocks, LANE // SUB, f2_total)
    out = jax.ShapeDtypeStruct((lines, HALF), F32)
    return pl.pallas_call(
        dft_kernel,
        out_shape=(out, out),
        cost_estimate=pl.CostEstimate(
            flops=2 * 3 * (2 * blocks * blocks * width + 4 * f2_total * width * blocks * LANE // SUB),
            bytes_accessed=4 * (blocks * width + 2 * lines * HALF + 2 * blocks * LANE) + 2 * 4 * blocks * blocks,
            transcendentals=0,
        ),
    )(x, *tables)


def body(velocity, new_owner, box_block, box_count, box_level):
    owners = lax.axis_size("own")
    groups = lax.axis_size("bulk")
    slot_total = velocity.shape[3]
    per_pair = slot_total // owners
    parcel_rows = owners * per_pair
    held_blocks = slot_total // 2
    first_block = lax.axis_index("bulk") * held_blocks
    slot_ids = jnp.arange(slot_total, dtype=jnp.int32)
    destination = new_owner[0, 0]
    filled = slot_ids < box_count[0, 0]
    same_owner = filled[:, None] & filled[None, :] & (destination[:, None] == destination[None, :])
    order_rank = jnp.sum((same_owner & (slot_ids[None, :] < slot_ids[:, None])).astype(jnp.int32), axis=1)
    row_of = jnp.where(filled, order_rank * owners + destination, parcel_rows)
    parcel_ids = jnp.arange(parcel_rows, dtype=jnp.int32)
    match = row_of[None, :] == parcel_ids[:, None]
    factor = level_factor(box_level[0, 0])
    source_safe = jnp.sum(jnp.where(match, slot_ids[None, :], 0), axis=1)
    row_factor = jnp.sum(jnp.where(match, factor[None, :], 0.0), axis=1)
    row_block = jnp.sum(jnp.where(match, box_block[0, 0][None, :] + 1, 0), axis=1) - 1
    code_lanes = jnp.arange(CODE_W, dtype=jnp.int32)
    by_owner = row_block.reshape(per_pair, owners).T
    codes = jnp.where(
        code_lanes[None, :] < per_pair,
        jnp.take(by_owner, jnp.minimum(code_lanes, per_pair - 1), axis=1),
        -1,
    ).astype(F32)

    parcel = source_divergence(velocity[:, 0, 0], source_safe, row_factor, codes, groups)

    arrived = lax.all_to_all(parcel, ("bulk", "own"), split_axis=0, concat_axis=0, tiled=True)
    piece_w = BOX * FACE // groups
    data_w = piece_w * per_pair
    code_in = arrived[:, data_w:data_w + per_pair].reshape(-1)
    total_blocks = groups * held_blocks
    place_at = jnp.where(code_in >= 0, code_in.astype(jnp.int32), total_blocks)
    arrived_ids = jnp.arange(code_in.shape[0], dtype=jnp.int32)
    block_ids = jnp.arange(total_blocks, dtype=jnp.int32)
    chosen = jnp.sum(jnp.where(place_at[None, :] == block_ids[:, None], arrived_ids[None, :], 0), axis=1)
    pieces = arrived[:, :data_w].reshape(-1, piece_w)
    cosine, sine_vals = line_spectra(jnp.take(pieces, chosen, axis=0, mode="clip"))
    return (cosine[None], sine_vals[None])


def solution(mesh):
    in_specs = (
        P(None, "bulk", "own", None, None),
        P("bulk", "own", None),
        P("bulk", "own", None),
        P("bulk", "own"),
        P("bulk", "own", None),
    )
    out_specs = (P("own", "bulk", None), P("own", "bulk", None))
    return jax.shard_map(body, mesh=mesh, in_specs=in_specs, out_specs=out_specs, check_vma=False)
```

```python
import math

import ml_dtypes
import numpy as np

import jax
import jax.numpy as jnp
from jax import lax
from jax.experimental import pallas as pl
from jax.experimental.pallas import tpu as pltpu
from jax.sharding import PartitionSpec as P

BOX = 16
GHOST = BOX + 2
PLANE = GHOST * GHOST
PLANE_PAD = 384
FACE = BOX * BOX
HALF = 3072
NX = 6144
SUB = 16
CODE_W = 128

HIGHEST = lax.Precision.HIGHEST
F32 = jnp.float32
BF16 = jnp.bfloat16


def level_factor(level):
    return jnp.where(level == 1, 0.5, jnp.where(level == 2, 1.0, 2.0)).astype(jnp.float32)


def selection_table():
    sel = np.zeros((PLANE_PAD, FACE), np.float32)
    for j in range(BOX):
        for k in range(BOX):
            sel[GHOST * (j + 1) + k + 1, j * BOX + k] = 1.0
    return jnp.asarray(sel, BF16)


def _split2(x):
    hi = x.astype(BF16)
    lo = (x - hi.astype(F32)).astype(BF16)
    return hi, lo


def _split3(x):
    hi = x.astype(BF16)
    rest = x - hi.astype(F32)
    mid = rest.astype(BF16)
    lo = (rest - mid.astype(F32)).astype(BF16)
    return hi, mid, lo


def _dot(a, b):
    return jnp.dot(a, b, preferred_element_type=F32)


def _exact_right(x, m):
    hi, mid, lo = _split3(x)
    return _dot(hi, m) + _dot(mid, m) + _dot(lo, m)


def _exact_left(m, x):
    hi, mid, lo = _split3(x)
    return _dot(m, hi) + _dot(m, mid) + _dot(m, lo)


WINDOW = 512
ROW_PAD = 6016


def _plane(x_ref, field, p):
    start = PLANE * p
    base = (start // 128) * 128
    off = start - base
    w = x_ref[field, :, base:base + WINDOW]
    if off:
        w = pltpu.roll(w, WINDOW - off, 1)
    return w[:, :PLANE_PAD]


TAIL_BASE = 5376


def divergence_kernel(src_ref, x_hbm, tail_hbm, sel_ref, fac_ref, code_ref, o_ref, buf, buf_tail, sem):
    owners = code_ref.shape[0]
    per_pair = src_ref.shape[0] // owners
    chunk_rows = o_ref.shape[0]
    data_w = o_ref.shape[1] - code_ref.shape[1]
    groups = chunk_rows // owners
    planes_per_group = BOX // groups
    piece_w = data_w // per_pair

    def fetch(t, slot):
        for r in range(owners):
            row = src_ref[t * owners + r]
            pltpu.make_async_copy(
                x_hbm.at[:, pl.ds(row, 1), :], buf.at[slot, :, pl.ds(r, 1), :], sem.at[slot, 0]
            ).start()
            pltpu.make_async_copy(
                tail_hbm.at[pl.ds(row, 1), :], buf_tail.at[slot, pl.ds(r, 1), :], sem.at[slot, 1]
            ).start()

    def wait(slot):
        pltpu.make_async_copy(x_hbm.at[:, pl.ds(0, owners), :], buf.at[slot], sem.at[slot, 0]).wait()
        pltpu.make_async_copy(tail_hbm.at[pl.ds(0, owners), :], buf_tail.at[slot], sem.at[slot, 1]).wait()

    fetch(0, 0)
    for g in range(groups):
        o_ref[g * owners:(g + 1) * owners, data_w:] = code_ref[...]
    sel = sel_ref[...]
    last = GHOST - 1
    for t in range(per_pair):
        slot = t % 2
        if t + 1 < per_pair:
            fetch(t + 1, 1 - slot)
        wait(slot)
        x_ref = buf.at[slot]
        v_planes = [_plane(x_ref, 1, p) for p in range(last)]
        tail = pltpu.roll(buf_tail[slot], WINDOW - (PLANE * last - TAIL_BASE), 1)
        v_planes.append(tail[:, :PLANE_PAD])
        pieces = []
        for i in range(BOX):
            u = _plane(x_ref, 0, i + 1)
            w = _plane(x_ref, 2, i + 1)
            along_x = pltpu.roll(u, PLANE_PAD - 1, 1) - pltpu.roll(u, 1, 1)
            along_y = v_planes[i + 2] - v_planes[i]
            along_z = pltpu.roll(w, PLANE_PAD - GHOST, 1) - pltpu.roll(w, GHOST, 1)
            pieces.append(along_x + (along_y + along_z))
        interior = _exact_right(jnp.concatenate(pieces, axis=0), sel)
        fac = fac_ref[t * owners:(t + 1) * owners, :]
        for i in range(BOX):
            g, half = divmod(i, planes_per_group)
            lane0 = t * piece_w + half * FACE
            o_ref[g * owners:(g + 1) * owners, lane0:lane0 + FACE] = interior[i * owners:(i + 1) * owners] * fac


def source_divergence(cells, source, factor, codes, groups):
    slots = cells.shape[1]
    owners = codes.shape[0]
    out_w = BOX * FACE // groups * (slots // owners) + CODE_W
    sel = selection_table()
    tail = jnp.pad(cells[1, :, TAIL_BASE:], ((0, 0), (0, TAIL_BASE + WINDOW - cells.shape[-1])))
    vmem = pl.BlockSpec(memory_space=pltpu.VMEM)
    return pl.pallas_call(
        divergence_kernel,
        in_specs=[
            pl.BlockSpec(memory_space=pltpu.SMEM),
            pl.BlockSpec(memory_space=pl.ANY),
            pl.BlockSpec(memory_space=pl.ANY),
            vmem,
            vmem,
            vmem,
        ],
        out_specs=vmem,
        out_shape=jax.ShapeDtypeStruct((groups * owners, out_w), F32),
        scratch_shapes=[
            pltpu.VMEM((2, 3, owners, cells.shape[2]), F32),
            pltpu.VMEM((2, owners, WINDOW), F32),
            pltpu.SemaphoreType.DMA((2, 2)),
        ],
        cost_estimate=pl.CostEstimate(
            flops=2 * slots * BOX * PLANE_PAD * FACE * 3,
            bytes_accessed=4 * (3 * slots * ROW_PAD + groups * owners * out_w),
            transcendentals=0,
        ),
    )(source, cells, tail, sel, jnp.broadcast_to(factor[:, None], (slots, FACE)), codes)


def _split_np(t):
    hi = t.astype(ml_dtypes.bfloat16)
    lo = (t - hi.astype(np.float64)).astype(ml_dtypes.bfloat16)
    return jnp.asarray(hi), jnp.asarray(lo)


def _angles(product, period):
    return (2.0 * np.pi / period) * (product % period).astype(np.float64)


def dft_tables(blocks, lines_per_block, f2_total):
    g_ids = np.arange(blocks, dtype=np.int64)
    stage_one = _angles(g_ids[:, None] * g_ids[None, :], blocks)
    lanes = lines_per_block * SUB
    twist = _angles(g_ids[:, None] * (np.arange(lanes) % SUB)[None, :], NX)
    row = np.arange(f2_total * lines_per_block)
    col = np.arange(lanes)
    same_line = (row[:, None] % lines_per_block) == (col[None, :] // SUB)
    last = _angles((row[:, None] // lines_per_block) * (col[None, :] % SUB), SUB)
    return (
        *_split_np(np.concatenate([np.cos(stage_one), np.sin(stage_one)], axis=0)),
        jnp.asarray(np.cos(twist), F32),
        jnp.asarray(np.sin(twist), F32),
        *_split_np(np.concatenate([np.where(same_line, np.cos(last), 0.0), np.where(same_line, np.sin(last), 0.0)], axis=0)),
    )


def _mm3(a_hi, a_lo, b_hi, b_lo, dims=None):
    if dims is None:
        f = _dot
    else:
        f = lambda a, b: lax.dot_general(a, b, dims, preferred_element_type=F32)
    return f(a_hi, b_hi) + (f(a_hi, b_lo) + f(a_lo, b_hi))


NT = (((1,), (1,)), ((), ()))
LANE = 128


def dft_kernel(x_ref, cs1h, cs1l, twc_ref, tws_ref, bcsh, bcsl, cos_ref, sin_ref):
    xh, xl = _split2(x_ref[...])
    blocks = x_ref.shape[0]
    y = _mm3(cs1h[...], cs1l[...], xh, xl)
    y_re = y[:blocks]
    y_im = -y[blocks:]
    twc = twc_ref[...]
    tws = tws_ref[...]
    bcs_h, bcs_l = bcsh[...], bcsl[...]
    half_rows = bcs_h.shape[0] // 2
    norm_scale = 1.0 / math.sqrt(NX)
    lines_per_block = LANE // SUB
    for part in range(x_ref.shape[1] // LANE):
        cols = slice(part * LANE, (part + 1) * LANE)
        yr = y_re[:, cols]
        yi = y_im[:, cols]
        zrh, zrl = _split2(yr * twc + yi * tws)
        zih, zil = _split2(yi * twc - yr * tws)
        from_re = _mm3(bcs_h, bcs_l, zrh, zrl, NT)
        from_im = _mm3(bcs_h, bcs_l, zih, zil, NT)
        x_re = from_re[:half_rows] + from_im[half_rows:]
        x_neg_im = from_re[half_rows:] - from_im[:half_rows]
        rows = slice(part * lines_per_block, (part + 1) * lines_per_block)
        for f2 in range(cos_ref.shape[1] // blocks):
            picked = slice(f2 * lines_per_block, (f2 + 1) * lines_per_block)
            cos_ref[rows, f2 * blocks:(f2 + 1) * blocks] = x_re[picked] * norm_scale
            sin_ref[rows, f2 * blocks:(f2 + 1) * blocks] = x_neg_im[picked] * norm_scale


def line_spectra(x):
    blocks, width = x.shape
    lines = width // SUB
    f2_total = HALF // blocks
    tables = dft_tables(blocks, LANE // SUB, f2_total)
    out = jax.ShapeDtypeStruct((lines, HALF), F32)
    return pl.pallas_call(
        dft_kernel,
        out_shape=(out, out),
        cost_estimate=pl.CostEstimate(
            flops=2 * 3 * (2 * blocks * blocks * width + 4 * f2_total * width * blocks * LANE // SUB),
            bytes_accessed=4 * (blocks * width + 2 * lines * HALF + 2 * blocks * LANE) + 2 * 4 * blocks * blocks,
            transcendentals=0,
        ),
    )(x, *tables)


def body(velocity, new_owner, box_block, box_count, box_level):
    owners = lax.axis_size("own")
    groups = lax.axis_size("bulk")
    slot_total = velocity.shape[3]
    per_pair = slot_total // owners
    parcel_rows = owners * per_pair
    held_blocks = slot_total // 2
    first_block = lax.axis_index("bulk") * held_blocks
    slot_ids = jnp.arange(slot_total, dtype=jnp.int32)
    destination = new_owner[0, 0]
    filled = slot_ids < box_count[0, 0]
    same_owner = filled[:, None] & filled[None, :] & (destination[:, None] == destination[None, :])
    order_rank = jnp.sum((same_owner & (slot_ids[None, :] < slot_ids[:, None])).astype(jnp.int32), axis=1)
    row_of = jnp.where(filled, order_rank * owners + destination, parcel_rows)
    parcel_ids = jnp.arange(parcel_rows, dtype=jnp.int32)
    match = row_of[None, :] == parcel_ids[:, None]
    factor = level_factor(box_level[0, 0])
    source_safe = jnp.sum(jnp.where(match, slot_ids[None, :], 0), axis=1)
    row_factor = jnp.sum(jnp.where(match, factor[None, :], 0.0), axis=1)
    row_block = jnp.sum(jnp.where(match, box_block[0, 0][None, :] + 1, 0), axis=1) - 1
    code_lanes = jnp.arange(CODE_W, dtype=jnp.int32)
    by_owner = row_block.reshape(per_pair, owners).T
    codes = jnp.where(
        code_lanes[None, :] < per_pair,
        jnp.take(by_owner, jnp.minimum(code_lanes, per_pair - 1), axis=1),
        -1,
    ).astype(F32)

    parcel = source_divergence(velocity[:, 0, 0], source_safe, row_factor, codes, groups)

    arrived = lax.all_to_all(parcel, ("bulk", "own"), split_axis=0, concat_axis=0, tiled=True)
    piece_w = BOX * FACE // groups
    data_w = piece_w * per_pair
    code_in = arrived[:, data_w:data_w + per_pair].reshape(-1)
    total_blocks = groups * held_blocks
    place_at = jnp.where(code_in >= 0, code_in.astype(jnp.int32), total_blocks)
    arrived_ids = jnp.arange(code_in.shape[0], dtype=jnp.int32)
    block_ids = jnp.arange(total_blocks, dtype=jnp.int32)
    chosen = jnp.sum(jnp.where(place_at[None, :] == block_ids[:, None], arrived_ids[None, :], 0), axis=1)
    pieces = arrived[:, :data_w].reshape(-1, piece_w)
    cosine, sine_vals = line_spectra(jnp.take(pieces, chosen, axis=0, mode="clip"))
    return (cosine[None], sine_vals[None])


def solution(mesh):
    in_specs = (
        P(None, "bulk", "own", None, None),
        P("bulk", "own", None),
        P("bulk", "own", None),
        P("bulk", "own"),
        P("bulk", "own", None),
    )
    out_specs = (P("own", "bulk", None), P("own", "bulk", None))
    return jax.shard_map(body, mesh=mesh, in_specs=in_specs, out_specs=out_specs, check_vma=False)
```

```python
import math

import ml_dtypes
import numpy as np

import jax
import jax.numpy as jnp
from jax import lax
from jax.experimental import pallas as pl
from jax.experimental.pallas import tpu as pltpu
from jax.sharding import PartitionSpec as P

BOX = 16
GHOST = BOX + 2
PLANE = GHOST * GHOST
PLANE_PAD = 384
FACE = BOX * BOX
HALF = 3072
NX = 6144
SUB = 16
CODE_W = 128

HIGHEST = lax.Precision.HIGHEST
F32 = jnp.float32
BF16 = jnp.bfloat16


def level_factor(level):
    return jnp.where(level == 1, 0.5, jnp.where(level == 2, 1.0, 2.0)).astype(jnp.float32)


def selection_table():
    sel = np.zeros((PLANE_PAD, FACE), np.float32)
    for j in range(BOX):
        for k in range(BOX):
            sel[GHOST * (j + 1) + k + 1, j * BOX + k] = 1.0
    return jnp.asarray(sel, BF16)


def _split2(x):
    hi = x.astype(BF16)
    lo = (x - hi.astype(F32)).astype(BF16)
    return hi, lo


def _split3(x):
    hi = x.astype(BF16)
    rest = x - hi.astype(F32)
    mid = rest.astype(BF16)
    lo = (rest - mid.astype(F32)).astype(BF16)
    return hi, mid, lo


def _dot(a, b):
    return jnp.dot(a, b, preferred_element_type=F32)


def _exact_right(x, m):
    hi, mid, lo = _split3(x)
    return _dot(hi, m) + _dot(mid, m) + _dot(lo, m)


def _exact_left(m, x):
    hi, mid, lo = _split3(x)
    return _dot(m, hi) + _dot(m, mid) + _dot(m, lo)


WINDOW = 512
ROW_PAD = 6016


def _plane(x_ref, field, p):
    start = PLANE * p
    base = (start // 128) * 128
    off = start - base
    w = x_ref[field, :, base:base + WINDOW]
    if off:
        w = pltpu.roll(w, WINDOW - off, 1)
    return w[:, :PLANE_PAD]


TAIL_BASE = 5376


def divergence_kernel(src_ref, x_hbm, tail_hbm, sel_ref, fac_ref, code_ref, o_ref, buf, buf_tail, sem):
    owners = code_ref.shape[0]
    per_pair = src_ref.shape[0] // owners
    chunk_rows = o_ref.shape[0]
    data_w = o_ref.shape[1] - code_ref.shape[1]
    groups = chunk_rows // owners
    planes_per_group = BOX // groups
    piece_w = data_w // per_pair

    def fetch(t, slot):
        for r in range(owners):
            row = src_ref[t * owners + r]
            pltpu.make_async_copy(
                x_hbm.at[:, pl.ds(row, 1), :], buf.at[slot, :, pl.ds(r, 1), :], sem.at[slot, 0]
            ).start()
            pltpu.make_async_copy(
                tail_hbm.at[pl.ds(row, 1), :], buf_tail.at[slot, pl.ds(r, 1), :], sem.at[slot, 1]
            ).start()

    def wait(slot):
        pltpu.make_async_copy(x_hbm.at[:, pl.ds(0, owners), :], buf.at[slot], sem.at[slot, 0]).wait()
        pltpu.make_async_copy(tail_hbm.at[pl.ds(0, owners), :], buf_tail.at[slot], sem.at[slot, 1]).wait()

    fetch(0, 0)
    for g in range(groups):
        o_ref[g * owners:(g + 1) * owners, data_w:] = code_ref[...]
    sel = sel_ref[...]
    last = GHOST - 1
    for t in range(per_pair):
        slot = t % 2
        if t + 1 < per_pair:
            fetch(t + 1, 1 - slot)
        wait(slot)
        x_ref = buf.at[slot]
        v_planes = [_plane(x_ref, 1, p) for p in range(last)]
        tail = pltpu.roll(buf_tail[slot], WINDOW - (PLANE * last - TAIL_BASE), 1)
        v_planes.append(tail[:, :PLANE_PAD])
        pieces = []
        for i in range(BOX):
            u = _plane(x_ref, 0, i + 1)
            w = _plane(x_ref, 2, i + 1)
            along_x = pltpu.roll(u, PLANE_PAD - 1, 1) - pltpu.roll(u, 1, 1)
            along_y = v_planes[i + 2] - v_planes[i]
            along_z = pltpu.roll(w, PLANE_PAD - GHOST, 1) - pltpu.roll(w, GHOST, 1)
            pieces.append(along_x + (along_y + along_z))
        interior = _exact_right(jnp.concatenate(pieces, axis=0), sel)
        fac = fac_ref[t * owners:(t + 1) * owners, :]
        for i in range(BOX):
            g, half = divmod(i, planes_per_group)
            lane0 = t * piece_w + half * FACE
            o_ref[g * owners:(g + 1) * owners, lane0:lane0 + FACE] = interior[i * owners:(i + 1) * owners] * fac


def source_divergence(cells, source, factor, codes, groups):
    slots = cells.shape[1]
    owners = codes.shape[0]
    out_w = BOX * FACE // groups * (slots // owners) + CODE_W
    sel = selection_table()
    tail = jnp.pad(cells[1, :, TAIL_BASE:], ((0, 0), (0, TAIL_BASE + WINDOW - cells.shape[-1])))
    vmem = pl.BlockSpec(memory_space=pltpu.VMEM)
    return pl.pallas_call(
        divergence_kernel,
        in_specs=[
            pl.BlockSpec(memory_space=pltpu.SMEM),
            pl.BlockSpec(memory_space=pl.ANY),
            pl.BlockSpec(memory_space=pl.ANY),
            vmem,
            vmem,
            vmem,
        ],
        out_specs=vmem,
        out_shape=jax.ShapeDtypeStruct((groups * owners, out_w), F32),
        scratch_shapes=[
            pltpu.VMEM((2, 3, owners, cells.shape[2]), F32),
            pltpu.VMEM((2, owners, WINDOW), F32),
            pltpu.SemaphoreType.DMA((2, 2)),
        ],
        cost_estimate=pl.CostEstimate(
            flops=2 * slots * BOX * PLANE_PAD * FACE * 3,
            bytes_accessed=4 * (3 * slots * ROW_PAD + groups * owners * out_w),
            transcendentals=0,
        ),
    )(source, cells, tail, sel, factor[:, None], codes)


def _split_np(t):
    hi = t.astype(ml_dtypes.bfloat16)
    lo = (t - hi.astype(np.float64)).astype(ml_dtypes.bfloat16)
    return jnp.asarray(hi), jnp.asarray(lo)


def _angles(product, period):
    return (2.0 * np.pi / period) * (product % period).astype(np.float64)


def dft_tables(blocks, lines_per_block, f2_total):
    g_ids = np.arange(blocks, dtype=np.int64)
    stage_one = _angles(g_ids[:, None] * g_ids[None, :], blocks)
    lanes = lines_per_block * SUB
    twist = _angles(g_ids[:, None] * (np.arange(lanes) % SUB)[None, :], NX)
    row = np.arange(f2_total * lines_per_block)
    col = np.arange(lanes)
    same_line = (row[:, None] % lines_per_block) == (col[None, :] // SUB)
    last = _angles((row[:, None] // lines_per_block) * (col[None, :] % SUB), SUB)
    return (
        *_split_np(np.concatenate([np.cos(stage_one), np.sin(stage_one)], axis=0)),
        jnp.asarray(np.cos(twist), F32),
        jnp.asarray(np.sin(twist), F32),
        *_split_np(np.concatenate([np.where(same_line, np.cos(last), 0.0), np.where(same_line, np.sin(last), 0.0)], axis=0)),
    )


def _mm3(a_hi, a_lo, b_hi, b_lo, dims=None):
    if dims is None:
        f = _dot
    else:
        f = lambda a, b: lax.dot_general(a, b, dims, preferred_element_type=F32)
    return f(a_hi, b_hi) + (f(a_hi, b_lo) + f(a_lo, b_hi))


NT = (((1,), (1,)), ((), ()))
LANE = 128


def dft_kernel(x_ref, cs1h, cs1l, twc_ref, tws_ref, bcsh, bcsl, cos_ref, sin_ref):
    xh, xl = _split2(x_ref[...])
    blocks = x_ref.shape[0]
    y = _mm3(cs1h[...], cs1l[...], xh, xl)
    y_re = y[:blocks]
    y_im = -y[blocks:]
    twc = twc_ref[...]
    tws = tws_ref[...]
    bcs_h, bcs_l = bcsh[...], bcsl[...]
    half_rows = bcs_h.shape[0] // 2
    norm_scale = 1.0 / math.sqrt(NX)
    lines_per_block = LANE // SUB
    for part in range(x_ref.shape[1] // LANE):
        cols = slice(part * LANE, (part + 1) * LANE)
        yr = y_re[:, cols]
        yi = y_im[:, cols]
        zrh, zrl = _split2(yr * twc + yi * tws)
        zih, zil = _split2(yi * twc - yr * tws)
        from_re = _mm3(bcs_h, bcs_l, zrh, zrl, NT)
        from_im = _mm3(bcs_h, bcs_l, zih, zil, NT)
        x_re = from_re[:half_rows] + from_im[half_rows:]
        x_neg_im = from_re[half_rows:] - from_im[:half_rows]
        rows = slice(part * lines_per_block, (part + 1) * lines_per_block)
        for f2 in range(cos_ref.shape[1] // blocks):
            picked = slice(f2 * lines_per_block, (f2 + 1) * lines_per_block)
            cos_ref[rows, f2 * blocks:(f2 + 1) * blocks] = x_re[picked] * norm_scale
            sin_ref[rows, f2 * blocks:(f2 + 1) * blocks] = x_neg_im[picked] * norm_scale


def line_spectra(x):
    blocks, width = x.shape
    lines = width // SUB
    f2_total = HALF // blocks
    tables = dft_tables(blocks, LANE // SUB, f2_total)
    out = jax.ShapeDtypeStruct((lines, HALF), F32)
    return pl.pallas_call(
        dft_kernel,
        out_shape=(out, out),
        cost_estimate=pl.CostEstimate(
            flops=2 * 3 * (2 * blocks * blocks * width + 4 * f2_total * width * blocks * LANE // SUB),
            bytes_accessed=4 * (blocks * width + 2 * lines * HALF + 2 * blocks * LANE) + 2 * 4 * blocks * blocks,
            transcendentals=0,
        ),
    )(x, *tables)


def body(velocity, new_owner, box_block, box_count, box_level):
    owners = lax.axis_size("own")
    groups = lax.axis_size("bulk")
    slot_total = velocity.shape[3]
    per_pair = slot_total // owners
    parcel_rows = owners * per_pair
    held_blocks = slot_total // 2
    first_block = lax.axis_index("bulk") * held_blocks
    slot_ids = jnp.arange(slot_total, dtype=jnp.int32)
    destination = new_owner[0, 0]
    filled = slot_ids < box_count[0, 0]
    same_owner = filled[:, None] & filled[None, :] & (destination[:, None] == destination[None, :])
    order_rank = jnp.sum((same_owner & (slot_ids[None, :] < slot_ids[:, None])).astype(jnp.int32), axis=1)
    row_of = jnp.where(filled, order_rank * owners + destination, parcel_rows)
    parcel_ids = jnp.arange(parcel_rows, dtype=jnp.int32)
    match = row_of[None, :] == parcel_ids[:, None]
    factor = level_factor(box_level[0, 0])
    source_safe = jnp.sum(jnp.where(match, slot_ids[None, :], 0), axis=1)
    row_factor = jnp.sum(jnp.where(match, factor[None, :], 0.0), axis=1)
    row_block = jnp.sum(jnp.where(match, box_block[0, 0][None, :] + 1, 0), axis=1) - 1
    code_lanes = jnp.arange(CODE_W, dtype=jnp.int32)
    by_owner = row_block.reshape(per_pair, owners).T
    codes = jnp.where(
        code_lanes[None, :] < per_pair,
        jnp.take(by_owner, jnp.minimum(code_lanes, per_pair - 1), axis=1),
        -1,
    ).astype(F32)

    parcel = source_divergence(velocity[:, 0, 0], source_safe, row_factor, codes, groups)

    arrived = lax.all_to_all(parcel, ("bulk", "own"), split_axis=0, concat_axis=0, tiled=True)
    piece_w = BOX * FACE // groups
    data_w = piece_w * per_pair
    code_in = arrived[:, data_w:data_w + per_pair].reshape(-1)
    total_blocks = groups * held_blocks
    place_at = jnp.where(code_in >= 0, code_in.astype(jnp.int32), total_blocks)
    arrived_ids = jnp.arange(code_in.shape[0], dtype=jnp.int32)
    block_ids = jnp.arange(total_blocks, dtype=jnp.int32)
    chosen = jnp.sum(jnp.where(place_at[None, :] == block_ids[:, None], arrived_ids[None, :], 0), axis=1)
    pieces = arrived[:, :data_w].reshape(-1, piece_w)
    cosine, sine_vals = line_spectra(jnp.take(pieces, chosen, axis=0, mode="clip"))
    return (cosine[None], sine_vals[None])


def solution(mesh):
    in_specs = (
        P(None, "bulk", "own", None, None),
        P("bulk", "own", None),
        P("bulk", "own", None),
        P("bulk", "own"),
        P("bulk", "own", None),
    )
    out_specs = (P("own", "bulk", None), P("own", "bulk", None))
    return jax.shard_map(body, mesh=mesh, in_specs=in_specs, out_specs=out_specs, check_vma=False)
```
